512 devices in a mesh: lat: 16 (over z, core), lon: 32 (over x, y).
Axes of the slice: x: 4, y: 8, z: 8, core: 2. Of those that a mesh axis runs over, the one named last changes fastest.
Arguments:
- fields: bfloat16 [2, 64, 640, 768], P(None, 'lat', None, 'lon'), may hold values from -6 to 6
- kernel: bfloat16 [5, 64, 3, 3, 64, 64], P(None, 'lat'), may hold values from -0.25 to 0.25
- band_low: int32 [5, 64], replicated, may hold values from -2 to 0
- block_shift: int32 [64, 3], replicated, may hold values from -3 to 3
- mix_weight: bfloat16 [5, 640, 640], P(None, 'lon'), may hold values from -0.109375 to 0.109375
Outputs:
- mixed: bfloat16 [2, 64, 768, 640], P(None, 'lat', 'lon')
The draws below stay inside these ranges and needn't reach their ends.
All inputs are finite; a program needn't handle non-finite values.
Results may differ from the reference program's by a relative error of at most 0.005.
Values may be sent and summed in bfloat16 or wider, within the bound.
A program may use at most 128 MiB of HBM per device.

```python
import jax
import jax.numpy as jnp
from jax import lax

C = 640
K = 5
BL = 64
TAPS = 3
J = 3
E = 2
NLAT = 64
NLON = 768
NB = 12


def set_ends(values, own_key, smallest, high):
    longest = values.shape.index(max(values.shape))
    spots = []
    for shift in (0, 1):
        where = [jax.random.randint(jax.random.fold_in(own_key, axis), (), 0, length) for axis, length in enumerate(values.shape)]
        where[longest] = (where[longest] + shift) % values.shape[longest]
        spots.append(tuple(where))
    return values.at[spots[0]].set(smallest).at[spots[1]].set(high)


def block_levels(stream_key, shape, shards, low, largest):
    gain = 1.0
    for axis_at, blocks in shards:
        draws = jax.random.uniform(jax.random.fold_in(jax.random.fold_in(stream_key, 6), axis_at), (blocks,), jnp.float32, low / len(shards), largest / len(shards))
        gain = gain * jnp.repeat(jnp.exp(draws), shape[axis_at] // blocks).reshape((-1,) + (1,) * (len(shape) - 1 - axis_at))
    return gain


def normal_values(own_key, extent, spread, limit, cuts=(), held_as=jnp.bfloat16):
    values = jax.random.normal(own_key, extent, jnp.float32) * spread
    if len(cuts) > 0:
        values = block_levels(own_key, extent, cuts, -0.22, 0.18) * values
    return jnp.clip(values, min=-limit, max=limit).astype(held_as)


def setup_inputs(seed: int = 0) -> dict:
    key_list = jax.random.split(jax.random.key(seed), 6)
    return {
        "fields": normal_values(key_list[0], (E, NLAT, C, NLON), 1.0, 6.0, ((1, 16), (3, 32))),
        "kernel": normal_values(key_list[1], (K, NLAT, TAPS, J, BL, BL), (TAPS * J * BL) ** -0.5, 0.25, ((1, 16),)),
        "band_low": set_ends(jax.random.randint(key_list[2], (K, NLAT), -2, 1), jax.random.fold_in(key_list[2], 1), -2, 0).astype(jnp.int32),
        "block_shift": set_ends(jax.random.randint(key_list[3], (NLAT, J), -3, 4), jax.random.fold_in(key_list[3], 1), -3, 3).astype(jnp.int32),
        "mix_weight": normal_values(key_list[4], (K, C, C), (K * C) ** -0.5, 0.109375, ((1, 32),)),
    }


def reference(fields, kernel, band_low, block_shift, mix_weight):
    blocks = fields.reshape(E, NLAT, C, NB, BL)
    lane_ids = jnp.arange(NB, dtype=jnp.int32)
    tap_ids = jnp.arange(TAPS, dtype=jnp.int32)
    weight_mix = mix_weight.astype(jnp.float32)

    def one_row(out_row):
        total = jnp.zeros((K, E, C, NB, BL), jnp.float32)
        for delta in range(-2, 3):
            source = out_row + delta
            valid = (source >= 0) & (source < NLAT)
            row_id = jnp.clip(source, 0, NLAT - 1).astype(jnp.int32)
            source_row = lax.dynamic_index_in_dim(blocks, row_id, 1, keepdims=False)
            shifts = lax.dynamic_index_in_dim(block_shift, row_id, 0, keepdims=False)
            index = (lane_ids[None, :] + shifts[:, None]) % NB
            picked = jnp.take(source_row, index, axis=2)
            kernel_row = lax.dynamic_index_in_dim(kernel, row_id, 1, keepdims=False)
            lows = lax.dynamic_index_in_dim(band_low, row_id, 1, keepdims=False)
            target = row_id + lows[:, None] + tap_ids[None, :]
            select = ((target == out_row) & valid).astype(jnp.float32)
            effective = jnp.einsum('kt,ktjpq->kjpq', select, kernel_row.astype(jnp.float32))
            total = total + jnp.einsum('ecjbp,kjpq->kecbq', picked.astype(jnp.float32), effective)
        conv = total.astype(jnp.bfloat16).reshape(K, E, C, NLON)
        summed = jnp.einsum('kecn,kcd->end', conv.astype(jnp.float32), weight_mix)
        return jax.nn.gelu(summed, approximate=False).astype(jnp.bfloat16)

    result = lax.map(one_row, jnp.arange(NLAT, dtype=jnp.int32))
    return jnp.transpose(result, (1, 0, 2, 3))
```

```python
import jax
import jax.numpy as jnp
from jax import lax
from jax.experimental import pallas as pl
from jax.experimental.pallas import tpu as pltpu
from jax.sharding import PartitionSpec as P

MESH = pl.DeviceIdType.MESH
F32 = jnp.float32
BF16 = jnp.bfloat16
NLAT, NLON = 16, 32


def pack_kernel(f_ref, w_ref, m_ref, wp_ref):
    rows = [f_ref[:, r].astype(F32).reshape(48, 640) for r in range(4)]
    gap = jnp.zeros((48, 48), F32)
    for g in range(16):
        cut = [row[:, 40 * g : 40 * g + 40] for row in rows]
        packed = jnp.concatenate([cut[0], cut[1], gap, cut[2], cut[3], gap], axis=1)
        m_ref[g] = packed.reshape(2, 24, 256).astype(BF16)
    odd = lax.rem(lax.axis_index("lon"), 2) == 1
    four = jnp.zeros((4, 640), F32)
    for k in range(5):
        w = w_ref[k].astype(F32)
        padded = jnp.where(
            odd,
            jnp.concatenate([four, w], axis=0),
            jnp.concatenate([w, four], axis=0),
        )
        wp_ref[3 * k : 3 * k + 3] = padded.reshape(3, 8, 640).astype(BF16)
    wp_ref[15] = jnp.zeros((8, 640), BF16)


def remote(src, dst, send, recv, where):
    return pltpu.make_async_remote_copy(
        src_ref=src,
        dst_ref=dst,
        send_sem=send,
        recv_sem=recv,
        device_id=where,
        device_id_type=MESH,
    )


def spread_kernel(
    m_ref, wp_ref, k_ref, r_ref, kh_ref, g_ref,
    m_send, m_recv, w_send, w_recv, h_send, h_recv, k_send, k_recv, own_sem,
):
    lat = lax.axis_index("lat")
    lon = lax.axis_index("lon")
    up = lax.rem(lat + 1, NLAT)
    down = lax.rem(lat + NLAT - 1, NLAT)
    barrier = pltpu.get_barrier_semaphore()

    def greet(j, c):
        pl.semaphore_signal(
            barrier, inc=1, device_id={"lon": lax.rem(lon + j, NLON)}, device_id_type=MESH
        )
        return c

    lax.fori_loop(1, NLON, greet, 0)
    pl.semaphore_signal(barrier, inc=1, device_id={"lat": up}, device_id_type=MESH)
    pl.semaphore_signal(barrier, inc=1, device_id={"lat": down}, device_id_type=MESH)
    pl.semaphore_wait(barrier, NLON + 1)

    own_m = pltpu.make_async_copy(m_ref.at[lon], r_ref.at[1, lon], own_sem.at[0])
    own_w = pltpu.make_async_copy(wp_ref.at[lat], g_ref.at[lon], own_sem.at[1])
    own_m.start()
    own_w.start()

    def send_m(j):
        to = lax.rem(lon + j, NLON)
        return remote(
            m_ref.at[to], r_ref.at[1, lon], m_send.at[to], m_recv.at[lon], {"lon": to}
        )

    def send_w(j):
        to = lax.rem(lon + j, NLON)
        return remote(
            wp_ref.at[lat], g_ref.at[lon], w_send.at[to], w_recv.at[lon], {"lon": to}
        )

    def start_m(j, c):
        send_m(j).start()
        return c

    def start_w(j, c):
        send_w(j).start()
        return c

    lax.fori_loop(1, NLON, start_m, 0)
    k_down = remote(
        k_ref.at[:, pl.ds(0, 2)], kh_ref.at[1], k_send.at[0], k_recv.at[0], {"lat": down}
    )
    k_up = remote(
        k_ref.at[:, pl.ds(2, 2)], kh_ref.at[0], k_send.at[1], k_recv.at[1], {"lat": up}
    )
    k_down.start()
    k_up.start()
    lax.fori_loop(1, NLON, start_w, 0)

    def take_m(j, c):
        src = lax.rem(lon + NLON - j, NLON)
        remote(
            m_ref.at[lon], r_ref.at[1, src], m_send.at[src], m_recv.at[src], {"lon": src}
        ).wait_recv()
        return c

    own_m.wait()
    lax.fori_loop(1, NLON, take_m, 0)
    h_down = remote(
        r_ref.at[1, :, :, pl.ds(0, 128)], r_ref.at[2, :, :, pl.ds(0, 128)],
        h_send.at[0], h_recv.at[0], {"lat": down},
    )
    h_up = remote(
        r_ref.at[1, :, :, pl.ds(128, 128)], r_ref.at[0, :, :, pl.ds(128, 128)],
        h_send.at[1], h_recv.at[1], {"lat": up},
    )
    h_down.start()
    h_up.start()

    def take_w(j, c):
        src = lax.rem(lon + NLON - j, NLON)
        remote(
            wp_ref.at[lat], g_ref.at[src], w_send.at[src], w_recv.at[src], {"lon": src}
        ).wait_recv()
        return c

    own_w.wait()
    lax.fori_loop(1, NLON, take_w, 0)

    def sent(j, c):
        send_m(j).wait_send()
        send_w(j).wait_send()
        return c

    lax.fori_loop(1, NLON, sent, 0)
    k_down.wait()
    k_up.wait()
    h_down.wait()
    h_up.wait()


ROWS = ((0, 2), (0, 3), (1, 0), (1, 1), (1, 2), (1, 3), (2, 0), (2, 1))


def conv_kernel(
    low_ref, shift_ref, r_ref, k_ref, kh_ref, a_ref, x_ref, lhs_ref, rhs_ref, acc_ref, sp_ref
):
    lat = lax.axis_index("lat")
    first = 4 * lat - 2
    half = lax.broadcasted_iota(jnp.int32, (80, 128), 1) < 64

    q = lax.broadcasted_iota(jnp.int32, (64, 256), 0)
    lane = lax.broadcasted_iota(jnp.int32, (64, 256), 1)
    base = 32 * (q >> 3) + (q & 7)
    for o in range(4):
        sp_ref[o] = jnp.where(lane == base + 8 * o, 1.0, 0.0).astype(BF16)
    sp_ref[4] = jnp.zeros((64, 256), BF16)

    for s, pairs in ((0, (1,)), (1, (0, 1)), (2, (0,))):
        for h in pairs:

            def turn(p, c, s=s, h=h):
                rows = pl.ds(pl.multiple_of(128 * p, 128), 128)
                t = r_ref[s, rows, 128 * h : 128 * h + 128].astype(F32).T[0:80]
                u = pltpu.roll(t, 64, 1)
                x_ref[s, 2 * p, 80 * h : 80 * h + 80] = jnp.where(half, t, u)
                x_ref[s, 2 * p + 1, 80 * h : 80 * h + 80] = jnp.where(half, u, t)
                return c

            lax.fori_loop(0, 6, turn, 0)

    left = lax.broadcasted_iota(jnp.int32, (40, 128), 1) < 64
    for i, (s, r) in enumerate(ROWS):
        row = jnp.clip(first + i, 0, 63)
        shifts = [shift_ref[row, j] for j in range(3)]

        def gather(p, c, i=i, s=s, r=r, shifts=shifts):
            out = []
            for b in range(2):
                blocks = [lax.rem(2 * p + b + sh + 12, 12) for sh in shifts]
                x0, x1, x2 = [x_ref[s, n, 40 * r : 40 * r + 40] for n in blocks]
                out.append(jnp.concatenate([jnp.where(left, x0, x1), x2], axis=1))
            rows = pl.ds(pl.multiple_of(80 * p, 16), 80)
            lhs_ref[rows, 256 * i : 256 * i + 256] = jnp.concatenate(out, axis=0).astype(BF16)
            return c

        lax.fori_loop(0, 6, gather, 0)
        rhs_ref[256 * i + 192 : 256 * i + 256] = jnp.zeros((64, 256), BF16)

    def basis(k, c):
        for i, (s, r) in enumerate(ROWS):
            row = first + i
            low = low_ref[k, jnp.clip(row, 0, 63)]
            total = jnp.zeros((192, 256), F32)
            for t in range(3):
                o = i - 2 + low + t
                good = (o >= 0) & (o < 4) & (row >= 0) & (row < 64)
                slot = jnp.where(good, o, 4)
                if s == 1:
                    weights = k_ref[k, r, t]
                else:
                    weights = kh_ref[s // 2, k, r % 2, t]
                total = total + jnp.dot(
                    weights.reshape(192, 64), sp_ref[slot], preferred_element_type=F32
                )
            rhs_ref[256 * i : 256 * i + 192] = total.astype(BF16)
        acc_ref[k] = jnp.dot(lhs_ref[...], rhs_ref[...], preferred_element_type=F32)
        return c

    lax.fori_loop(0, 5, basis, 0)

    tail = jnp.zeros((40, 32), F32)
    for y in range(8):
        groups = [divmod(3 * y + n, 8) for n in range(3)]
        for x in range(4):
            parts = []
            for k in range(5):
                n = 0
                while n < 3:
                    beta, qg = groups[n]
                    m = n
                    while m < 3 and groups[m][0] == beta:
                        m += 1
                    rows = slice(40 * (3 * x + beta), 40 * (3 * x + beta) + 40)
                    parts.append(acc_ref[k, rows, 32 * qg : 32 * (qg + m - n)])
                    n = m
            a_ref[x, y] = jnp.concatenate(parts + [tail], axis=1).astype(BF16)


def return_kernel(
    a_ref, g_ref, ra_ref, ga_ref, a_send, a_recv, c_send, c_recv, s_send, s_recv, own_sem
):
    lat = lax.axis_index("lat")
    lon = lax.axis_index("lon")
    up = lax.rem(lat + 2, NLAT)
    down = lax.rem(lat + NLAT - 2, NLAT)
    twin = lat + 1 - 2 * lax.rem(lat, 2)
    barrier = pltpu.get_barrier_semaphore()

    def greet(j, c):
        pl.semaphore_signal(
            barrier, inc=1, device_id={"lon": lax.rem(lon + j, NLON)}, device_id_type=MESH
        )
        return c

    lax.fori_loop(1, NLON, greet, 0)
    for other in (up, down, twin):
        pl.semaphore_signal(barrier, inc=1, device_id={"lat": other}, device_id_type=MESH)
    pl.semaphore_wait(barrier, NLON + 2)

    def piece_up(n, base):
        return lax.rem(base + 2 * NLAT - 2 * n, NLAT)

    def piece_down(n, base):
        return lax.rem(base + 2 * n, NLAT)

    started = []

    def go(copy):
        copy.start()
        started.append(copy)

    def ring_up(n):
        src = g_ref if n == 0 else ga_ref.at[piece_up(n, lat)]
        return remote(
            src, ga_ref.at[piece_up(n, lat)], c_send.at[n], c_recv.at[n], {"lat": up}
        )

    def ring_down(n):
        src = g_ref if n == 0 else ga_ref.at[piece_down(n, lat)]
        return remote(
            src, ga_ref.at[piece_down(n, lat)], c_send.at[4 + n], c_recv.at[4 + n], {"lat": down}
        )

    def to_twin(slot, piece, src):
        return remote(
            src, ga_ref.at[piece], s_send.at[slot], s_recv.at[slot], {"lat": twin}
        )

    go(ring_up(0))
    go(ring_down(0))

    def send_a(j):
        to = lax.rem(lon + j, NLON)
        return remote(
            a_ref.at[to], ra_ref.at[lon], a_send.at[to], a_recv.at[lon], {"lon": to}
        )

    def start_a(j, c):
        send_a(j).start()
        return c

    lax.fori_loop(1, NLON, start_a, 0)
    own_a = pltpu.make_async_copy(a_ref.at[lon], ra_ref.at[lon], own_sem.at[0])
    own_g = pltpu.make_async_copy(g_ref, ga_ref.at[lat], own_sem.at[1])
    own_a.start()
    own_g.start()
    go(to_twin(0, lat, g_ref))

    for n in range(1, 5):
        piece = piece_up(n, lat)
        remote(
            g_ref, ga_ref.at[piece], c_send.at[n - 1], c_recv.at[n - 1], {"lat": up}
        ).wait_recv()
        if n < 4:
            go(ring_up(n))
        go(to_twin(n, piece, ga_ref.at[piece]))
        if n < 4:
            piece = piece_down(n, lat)
            remote(
                g_ref, ga_ref.at[piece], c_send.at[3 + n], c_recv.at[3 + n], {"lat": down}
            ).wait_recv()
            if n < 3:
                go(ring_down(n))
            go(to_twin(4 + n, piece, ga_ref.at[piece]))

    def take_a(j, c):
        src = lax.rem(lon + NLON - j, NLON)
        remote(
            a_ref.at[lon], ra_ref.at[src], a_send.at[src], a_recv.at[src], {"lon": src}
        ).wait_recv()
        send_a(j).wait_send()
        return c

    lax.fori_loop(1, NLON, take_a, 0)
    for slot in range(8):
        piece = piece_up(slot, twin) if slot < 5 else piece_down(slot - 4, twin)
        remote(
            g_ref, ga_ref.at[piece], s_send.at[slot], s_recv.at[slot], {"lat": twin}
        ).wait_recv()
    for copy in started:
        copy.wait_send()
    own_a.wait()
    own_g.wait()


def mix_kernel(ra_ref, g_ref, o_ref, t_ref, acc_ref):
    k = pl.program_id(0)

    @pl.when(k == 0)
    def _():
        for e in range(2):
            a = ra_ref[:, e].astype(F32).reshape(640, 512)
            t_ref[e] = a.T.astype(BF16)
        acc_ref[...] = jnp.zeros_like(acc_ref)

    def part(r, h):
        return g_ref[r, :, h].astype(F32)

    w = jnp.stack(
        [part(0, 0), part(1, 0), part(2, 0) + part(0, 1), part(1, 1), part(2, 1)], axis=1
    )
    w = w.reshape(640, 640).astype(BF16)
    rows = pl.ds(pl.multiple_of(96 * k, 32), 96)
    for e in range(2):
        acc_ref[e] += jnp.dot(t_ref[e, rows], w, preferred_element_type=F32)

    @pl.when(k == 4)
    def _():
        for e in range(2):
            v = acc_ref[e].reshape(3, 4, 8, 640)
            v = v * (1.0 + lax.erf(v * 0.7071067811865476)) * 0.5
            for o in range(4):
                o_ref[e, o] = v[:, o].reshape(24, 640).astype(BF16)


def per_device(fields, kernel, band_low, block_shift, mix_weight):
    whole = pl.BlockSpec(memory_space=pltpu.VMEM)
    smem = pl.BlockSpec(memory_space=pltpu.SMEM)
    anywhere = pl.BlockSpec(memory_space=pl.ANY)
    shape = jax.ShapeDtypeStruct
    dma = pltpu.SemaphoreType.DMA

    cells_first = jnp.transpose(fields, (0, 1, 3, 2))
    messages, pieces = pl.pallas_call(
        pack_kernel,
        out_shape=(shape((16, 2, 24, 256), BF16), shape((16, 8, 640), BF16)),
        in_specs=[whole, whole],
        out_specs=(whole, whole),
        name="pack",
    )(cells_first, mix_weight)
    received, kernel_halo, gathered = pl.pallas_call(
        spread_kernel,
        out_shape=(
            shape((3, 32, 24, 256), BF16),
            shape((2, 5, 2, 3, 3, 64, 64), BF16),
            shape((32, 8, 640), BF16),
        ),
        in_specs=[anywhere] * 3,
        out_specs=(anywhere,) * 3,
        scratch_shapes=[
            dma((32,)), dma((32,)), dma((32,)), dma((32,)),
            dma((2,)), dma((2,)), dma((2,)), dma((2,)), dma((2,)),
        ],
        compiler_params=pltpu.CompilerParams(collective_id=0, has_side_effects=True),
        name="spread",
    )(messages.reshape(32, 24, 256), pieces, kernel)
    convolved = pl.pallas_call(
        conv_kernel,
        out_shape=shape((4, 8, 40, 512), BF16),
        in_specs=[smem, smem, whole, whole, whole],
        out_specs=whole,
        scratch_shapes=[
            pltpu.VMEM((3, 12, 160, 128), F32),
            pltpu.VMEM((480, 2048), BF16),
            pltpu.VMEM((2048, 256), BF16),
            pltpu.VMEM((5, 480, 256), F32),
            pltpu.VMEM((5, 64, 256), BF16),
        ],
        name="conv",
    )(band_low, block_shift, received.reshape(3, 768, 256), kernel, kernel_halo)
    returned, weights = pl.pallas_call(
        return_kernel,
        out_shape=(shape((32, 40, 512), BF16), shape((16, 32, 8, 640), BF16)),
        in_specs=[anywhere] * 2,
        out_specs=(anywhere,) * 2,
        scratch_shapes=[
            dma((32,)), dma((32,)), dma((7,)), dma((7,)), dma((8,)), dma((8,)), dma((2,)),
        ],
        compiler_params=pltpu.CompilerParams(collective_id=1, has_side_effects=True),
        name="give_back",
    )(convolved.reshape(32, 40, 512), gathered)
    return pl.pallas_call(
        mix_kernel,
        out_shape=shape((2, 4, 24, 640), BF16),
        grid=(5,),
        in_specs=[
            pl.BlockSpec((16, 2, 40, 512), lambda k: (0, 0, 0, 0)),
            pl.BlockSpec((3, 16, 2, 8, 640), lambda k: (k, 0, 0, 0, 0)),
        ],
        out_specs=pl.BlockSpec((2, 4, 24, 640), lambda k: (0, 0, 0, 0)),
        scratch_shapes=[pltpu.VMEM((2, 512, 640), BF16), pltpu.VMEM((2, 96, 640), F32)],
        name="mix",
    )(returned.reshape(16, 2, 40, 512), weights.reshape(16, 16, 2, 8, 640))


def solution(mesh):
    placed = (
        P(None, "lat", None, "lon"),
        P(None, "lat", None, None, None, None),
        P(),
        P(),
        P(None, "lon", None),
    )
    return jax.shard_map(
        per_device,
        mesh=mesh,
        in_specs=placed,
        out_specs=P(None, "lat", "lon", None),
        check_vma=False,
    )
```

```python
import jax
import jax.numpy as jnp
from jax import lax
from jax.experimental import pallas as pl
from jax.experimental.pallas import tpu as pltpu
from jax.sharding import PartitionSpec as P

MESH = pl.DeviceIdType.MESH
F32 = jnp.float32
BF16 = jnp.bfloat16
NLAT, NLON = 16, 32


def remote(src, dst, send, recv, where):
    return pltpu.make_async_remote_copy(
        src_ref=src,
        dst_ref=dst,
        send_sem=send,
        recv_sem=recv,
        device_id=where,
        device_id_type=MESH,
    )


def layer_kernel(
    low_ref, shift_ref, f_ref, w_ref, k_hbm, ra_ref, ga_ref,
    k_ref, m_ref, wp_ref, r_ref, rh_ref, g_ref, ku_ref, kh_ref,
    x_ref, lhs_ref, rhs_ref, acc_ref, a_ref, sp_ref, sq_ref,
    m_send, m_recv, w_send, w_recv, a_send, a_recv,
    h_send, h_recv, k_send, k_recv, c_send, c_recv, s_send, s_recv, own_sem,
):
    lat = lax.axis_index("lat")
    lon = lax.axis_index("lon")
    up, down = lax.rem(lat + 1, NLAT), lax.rem(lat + NLAT - 1, NLAT)
    up2, down2 = lax.rem(lat + 2, NLAT), lax.rem(lat + NLAT - 2, NLAT)
    twin = lat + 1 - 2 * lax.rem(lat, 2)
    first = 4 * lat
    barrier = pltpu.get_barrier_semaphore()

    def peer(j):
        return lax.rem(lon + j, NLON)

    def greet(j, c):
        pl.semaphore_signal(barrier, inc=1, device_id={"lon": peer(j)}, device_id_type=MESH)
        return c

    lax.fori_loop(1, NLON, greet, 0)
    for other in (up, down, up2, down2):
        pl.semaphore_signal(barrier, inc=1, device_id={"lat": other}, device_id_type=MESH)
    k_copy = pltpu.make_async_copy(k_hbm, k_ref, own_sem.at[0])
    k_copy.start()

    rows = [f_ref[:, r].astype(F32).reshape(48, 640) for r in range(4)]
    gap = jnp.zeros((48, 48), F32)
    for g in range(16):
        cut = [row[:, 40 * g : 40 * g + 40] for row in rows]
        packed = jnp.concatenate([cut[0], cut[1], gap, cut[2], cut[3], gap], axis=1)
        m_ref[2 * g] = packed[0:24].astype(BF16)
        m_ref[2 * g + 1] = packed[24:48].astype(BF16)
    odd = lax.rem(lon, 2) == 1
    four = jnp.zeros((4, 640), F32)
    for k in range(5):
        w = w_ref[k].astype(F32)
        padded = jnp.where(
            odd,
            jnp.concatenate([four, w], axis=0),
            jnp.concatenate([w, four], axis=0),
        )
        for n in range(3):
            wp_ref[3 * k + n] = padded[8 * n : 8 * n + 8].astype(BF16)
    wp_ref[15] = jnp.zeros((8, 640), BF16)

    q = lax.broadcasted_iota(jnp.int32, (64, 256), 0)
    lane = lax.broadcasted_iota(jnp.int32, (64, 256), 1)
    base = 32 * (q >> 3) + (q & 7)
    for o in range(4):
        spread = jnp.where(lane == base + 8 * o, 1.0, 0.0).astype(BF16)
        sp_ref[o] = spread
        sq_ref[o // 2, 64 * (o % 2) : 64 * (o % 2) + 64] = spread
    sp_ref[4] = jnp.zeros((64, 256), BF16)

    k_copy.wait()

    def pack_halo(k, c):
        for side in range(2):
            for n in range(2):
                r = 2 * (1 - side) + n
                low = low_ref[k, first + r]
                inside = (lat < NLAT - 1) if side == 0 else (lat > 0)
                halves = []
                for o in range(2):
                    t = o + 2 - n - low if side == 0 else o - 2 - n - low
                    good = (t >= 0) & (t < 3) & inside
                    block = k_ref[k, r, jnp.clip(t, 0, 2)].reshape(192, 64).astype(F32)
                    halves.append(jnp.where(good, block, 0.0))
                ku_ref[side, k, n] = jnp.concatenate(halves, axis=1).astype(BF16)
        return c

    lax.fori_loop(0, 5, pack_halo, 0)

    pl.semaphore_wait(barrier, NLON + 3)

    def send_m(j):
        to = peer(j)
        return remote(m_ref.at[to], r_ref.at[lon], m_send.at[to], m_recv.at[lon], {"lon": to})

    def send_w(j):
        to = peer(j)
        return remote(wp_ref.at[lat], g_ref.at[lon], w_send.at[to], w_recv.at[lon], {"lon": to})

    def send_a(to):
        return remote(a_ref.at[to], ra_ref.at[lon], a_send.at[to], a_recv.at[lon], {"lon": to})

    def start_m(j, c):
        send_m(j).start()
        return c

    def start_w(j, c):
        send_w(j).start()
        return c

    lax.fori_loop(1, NLON, start_m, 0)
    own_m = pltpu.make_async_copy(m_ref.at[lon], r_ref.at[lon], own_sem.at[1])
    own_w = pltpu.make_async_copy(wp_ref.at[lat], g_ref.at[lon], own_sem.at[2])
    own_m.start()
    own_w.start()
    k_up = remote(ku_ref.at[0], kh_ref.at[0], k_send.at[0], k_recv.at[0], {"lat": up})
    k_down = remote(ku_ref.at[1], kh_ref.at[1], k_send.at[1], k_recv.at[1], {"lat": down})
    k_up.start()
    k_down.start()
    lax.fori_loop(1, NLON, start_w, 0)

    def own_rows(k, c):
        for r in range(4):
            low = low_ref[k, first + r]
            total = jnp.zeros((192, 256), F32)
            for t in range(3):
                o = r + low + t
                slot = jnp.where((o >= 0) & (o < 4), o, 4)
                total = total + jnp.dot(
                    k_ref[k, r, t].reshape(192, 64), sp_ref[slot], preferred_element_type=F32
                )
            at = 256 * (r + 2)
            rhs_ref[k, at : at + 192] = total.astype(BF16)
        for i in range(8):
            rhs_ref[k, 256 * i + 192 : 256 * i + 256] = jnp.zeros((64, 256), BF16)
        return c

    lax.fori_loop(0, 5, own_rows, 0)

    def take_m(j, c):
        src = lax.rem(lon + NLON - j, NLON)
        remote(
            m_ref.at[lon], r_ref.at[src], m_send.at[src], m_recv.at[src], {"lon": src}
        ).wait_recv()
        return c

    own_m.wait()
    lax.fori_loop(1, NLON, take_m, 0)
    h_up = remote(
        r_ref.at[:, :, pl.ds(128, 128)], rh_ref.at[0], h_send.at[0], h_recv.at[0], {"lat": up}
    )
    h_down = remote(
        r_ref.at[:, :, pl.ds(0, 128)], rh_ref.at[1], h_send.at[1], h_recv.at[1], {"lat": down}
    )
    h_up.start()
    h_down.start()

    left80 = lax.broadcasted_iota(jnp.int32, (80, 128), 1) < 64
    left40 = lax.broadcasted_iota(jnp.int32, (40, 128), 1) < 64

    def turn(slot, load):
        for u in range(2):
            cells = load(16 * u).astype(F32).reshape(384, 128)
            for p in range(3):
                t = cells[128 * p : 128 * p + 128].T[0:80]
                s = pltpu.roll(t, 64, 1)
                x_ref[slot, 6 * u + 2 * p] = jnp.where(left80, t, s)
                x_ref[slot, 6 * u + 2 * p + 1] = jnp.where(left80, s, t)

    def gather(rows):
        for i in rows:
            row = jnp.clip(first - 2 + i, 0, 63)
            shifts = [shift_ref[j, row] + 12 for j in range(3)]
            part = slice(40 * (i % 2), 40 * (i % 2) + 40)

            def group(x, c, i=i, shifts=shifts, part=part):
                out = []
                for b in range(3):
                    x0, x1, x2 = [
                        x_ref[i // 2, lax.rem(3 * x + b + s, 12), part] for s in shifts
                    ]
                    out.append(jnp.concatenate([jnp.where(left40, x0, x1), x2], axis=1))
                lhs_ref[x, :, 256 * i : 256 * i + 256] = jnp.concatenate(out, axis=0).astype(BF16)
                return c

            lax.fori_loop(0, 4, group, 0)

    turn(1, lambda u: r_ref[u : u + 16, :, 0:128])
    turn(2, lambda u: r_ref[u : u + 16, :, 128:256])
    gather((2, 3, 4, 5))

    k_up.wait_recv()
    k_down.wait_recv()

    def halo_rows(k, c):
        for side in range(2):
            for n in range(2):
                at = 256 * (6 * side + n)
                rhs_ref[k, at : at + 192] = jnp.dot(
                    kh_ref[side, k, n], sq_ref[side], preferred_element_type=F32
                ).astype(BF16)
        return c

    lax.fori_loop(0, 5, halo_rows, 0)

    h_up.wait_recv()
    h_down.wait_recv()
    turn(0, lambda u: rh_ref[0, u : u + 16])
    turn(3, lambda u: rh_ref[1, u : u + 16])
    gather((0, 1, 6, 7))

    def above(n, start):
        return lax.rem(start + 2 * n, NLAT)

    def below(n, start):
        return lax.rem(start + 2 * NLAT - 2 * n, NLAT)

    started = []

    def go(copy):
        copy.start()
        started.append(copy)

    def ring_up(n):
        src = g_ref if n == 0 else ga_ref.at[below(n, lat)]
        return remote(
            src, ga_ref.at[below(n, lat)], c_send.at[n], c_recv.at[n], {"lat": up2}
        )

    def ring_down(n):
        src = g_ref if n == 0 else ga_ref.at[above(n, lat)]
        return remote(
            src, ga_ref.at[above(n, lat)], c_send.at[4 + n], c_recv.at[4 + n], {"lat": down2}
        )

    def to_twin(slot, piece, src):
        return remote(src, ga_ref.at[piece], s_send.at[slot], s_recv.at[slot], {"lat": twin})

    def ring_step(n):
        piece = below(n, lat)
        remote(
            g_ref, ga_ref.at[piece], c_send.at[n - 1], c_recv.at[n - 1], {"lat": up2}
        ).wait_recv()
        if n < 4:
            go(ring_up(n))
        go(to_twin(n, piece, ga_ref.at[piece]))
        if n < 4:
            piece = above(n, lat)
            remote(
                g_ref, ga_ref.at[piece], c_send.at[3 + n], c_recv.at[3 + n], {"lat": down2}
            ).wait_recv()
            if n < 3:
                go(ring_down(n))
            go(to_twin(4 + n, piece, ga_ref.at[piece]))

    def take_w(j, c):
        src = lax.rem(lon + NLON - j, NLON)
        remote(
            wp_ref.at[lat], g_ref.at[src], w_send.at[src], w_recv.at[src], {"lon": src}
        ).wait_recv()
        return c

    tail = jnp.zeros((40, 32), F32)
    own_x, own_y = lon // 8, lax.rem(lon, 8)
    own_a = pltpu.make_async_copy(a_ref.at[lon], ra_ref.at[lon], own_sem.at[3])
    own_g = pltpu.make_async_copy(g_ref, ga_ref.at[lat], own_sem.at[4])
    for step in range(4):
        x = lax.rem(own_x + step, 4)

        def basis(k, c, x=x):
            acc_ref[k] = jnp.dot(lhs_ref[x], rhs_ref[k], preferred_element_type=F32)
            return c

        lax.fori_loop(0, 5, basis, 0)
        for y in range(8):
            groups = [divmod(3 * y + n, 8) for n in range(3)]
            parts = []
            for k in range(5):
                n = 0
                while n < 3:
                    beta, qg = groups[n]
                    m = n
                    while m < 3 and groups[m][0] == beta:
                        m += 1
                    parts.append(
                        acc_ref[k, 40 * beta : 40 * beta + 40, 32 * qg : 32 * (qg + m - n)]
                    )
                    n = m
            a_ref[8 * x + y] = jnp.concatenate(parts + [tail], axis=1).astype(BF16)

        def start_a(n, c, x=x):
            send_a(8 * x + lax.rem(own_y + n, 8)).start()
            return c

        lax.fori_loop(1 if step == 0 else 0, 8, start_a, 0)
        if step == 0:
            own_a.start()
            own_w.wait()
            lax.fori_loop(1, NLON, take_w, 0)
            go(ring_up(0))
            go(ring_down(0))
            own_g.start()
            go(to_twin(0, lat, g_ref))
        elif step > 1:
            ring_step(step - 1)
    ring_step(3)
    ring_step(4)

    def finish(j, c):
        src = lax.rem(lon + NLON - j, NLON)
        remote(
            a_ref.at[lon], ra_ref.at[src], a_send.at[src], a_recv.at[src], {"lon": src}
        ).wait_recv()
        send_a(peer(j)).wait_send()
        send_m(j).wait_send()
        send_w(j).wait_send()
        return c

    lax.fori_loop(1, NLON, finish, 0)
    for slot in range(8):
        piece = below(slot, twin) if slot < 5 else above(slot - 4, twin)
        remote(
            g_ref, ga_ref.at[piece], s_send.at[slot], s_recv.at[slot], {"lat": twin}
        ).wait_recv()
    for copy in started + [k_up, k_down, h_up, h_down]:
        copy.wait_send()
    own_a.wait()
    own_g.wait()


def mix_kernel(ra_ref, g_ref, o_ref, t_ref, acc_ref):
    k = pl.program_id(0)

    @pl.when(k == 0)
    def _():
        for e in range(2):
            a = ra_ref[:, e].astype(F32).reshape(640, 512)
            t_ref[e] = a.T.astype(BF16)
        acc_ref[...] = jnp.zeros_like(acc_ref)

    def part(r, h):
        return g_ref[r, :, h].astype(F32)

    w = jnp.stack(
        [part(0, 0), part(1, 0), part(2, 0) + part(0, 1), part(1, 1), part(2, 1)], axis=1
    )
    w = w.reshape(640, 640).astype(BF16)
    rows = pl.ds(pl.multiple_of(96 * k, 32), 96)
    for e in range(2):
        acc_ref[e] += jnp.dot(t_ref[e, rows], w, preferred_element_type=F32)

    @pl.when(k == 4)
    def _():
        for e in range(2):
            v = acc_ref[e].reshape(3, 4, 8, 640)
            v = v * (1.0 + lax.erf(v * 0.7071067811865476)) * 0.5
            for o in range(4):
                o_ref[e, o] = v[:, o].reshape(24, 640).astype(BF16)


def per_device(fields, kernel, band_low, block_shift, mix_weight):
    whole = pl.BlockSpec(memory_space=pltpu.VMEM)
    smem = pl.BlockSpec(memory_space=pltpu.SMEM)
    anywhere = pl.BlockSpec(memory_space=pl.ANY)
    shape = jax.ShapeDtypeStruct
    dma = pltpu.SemaphoreType.DMA
    vmem = pltpu.VMEM

    returned, weights = pl.pallas_call(
        layer_kernel,
        out_shape=(shape((32, 40, 512), BF16), shape((16, 32, 8, 640), BF16)),
        in_specs=[smem, smem, whole, whole, anywhere],
        out_specs=(anywhere,) * 2,
        scratch_shapes=[
            vmem((5, 4, 3, 3, 64, 64), BF16),
            vmem((32, 24, 256), BF16),
            vmem((16, 8, 640), BF16),
            vmem((32, 24, 256), BF16),
            vmem((2, 32, 24, 128), BF16),
            vmem((32, 8, 640), BF16),
            vmem((2, 5, 2, 192, 128), BF16),
            vmem((2, 5, 2, 192, 128), BF16),
            vmem((4, 12, 80, 128), F32),
            vmem((4, 120, 2048), BF16),
            vmem((5, 2048, 256), BF16),
            vmem((5, 120, 256), F32),
            vmem((32, 40, 512), BF16),
            vmem((5, 64, 256), BF16),
            vmem((2, 128, 256), BF16),
            dma((32,)), dma((32,)), dma((32,)), dma((32,)), dma((32,)), dma((32,)),
            dma((2,)), dma((2,)), dma((2,)), dma((2,)),
            dma((7,)), dma((7,)), dma((8,)), dma((8,)), dma((5,)),
        ],
        compiler_params=pltpu.CompilerParams(collective_id=0, has_side_effects=True),
        name="layer",
    )(
        band_low,
        block_shift.T,
        jnp.transpose(fields, (0, 1, 3, 2)),
        mix_weight,
        kernel,
    )
    return pl.pallas_call(
        mix_kernel,
        out_shape=shape((2, 4, 24, 640), BF16),
        grid=(5,),
        in_specs=[
            pl.BlockSpec((16, 2, 40, 512), lambda k: (0, 0, 0, 0)),
            pl.BlockSpec((3, 16, 2, 8, 640), lambda k: (k, 0, 0, 0, 0)),
        ],
        out_specs=pl.BlockSpec((2, 4, 24, 640), lambda k: (0, 0, 0, 0)),
        scratch_shapes=[pltpu.VMEM((2, 512, 640), BF16), pltpu.VMEM((2, 96, 640), F32)],
        name="mix",
    )(returned.reshape(16, 2, 40, 512), weights.reshape(16, 16, 2, 8, 640))


def solution(mesh):
    placed = (
        P(None, "lat", None, "lon"),
        P(None, "lat", None, None, None, None),
        P(),
        P(),
        P(None, "lon", None),
    )
    return jax.shard_map(
        per_device,
        mesh=mesh,
        in_specs=placed,
        out_specs=P(None, "lat", "lon", None),
        check_vma=False,
    )
```

```python
import jax
import jax.numpy as jnp
from jax import lax
from jax.experimental import pallas as pl
from jax.experimental.pallas import tpu as pltpu
from jax.sharding import PartitionSpec as P

MESH = pl.DeviceIdType.MESH
F32 = jnp.float32
BF16 = jnp.bfloat16
NLAT, NLON = 16, 32


def remote(src, dst, send, recv, where):
    return pltpu.make_async_remote_copy(
        src_ref=src,
        dst_ref=dst,
        send_sem=send,
        recv_sem=recv,
        device_id=where,
        device_id_type=MESH,
    )


def layer_kernel(
    low_ref, shift_ref, f_hbm, w_hbm, k_hbm, o_ref,
    f_ref, w_ref, k_ref, m_ref, wp_ref, r_ref, rh_ref, g_ref, ku_ref, kh_ref,
    x_ref, lhs_ref, rhs_ref, acc_ref, a_ref, sp_ref, sq_ref,
    ra_ref, ga_ref, wv_ref, t_ref, sum_ref,
    m_send, m_recv, y_send, y_recv, b_send, b_recv, a_send, a_recv,
    h_send, h_recv, k_send, k_recv, c_send, c_recv, s_send, s_recv, own_sem,
):
    lat = lax.axis_index("lat")
    lon = lax.axis_index("lon")
    up, down = lax.rem(lat + 1, NLAT), lax.rem(lat + NLAT - 1, NLAT)
    up2, down2 = lax.rem(lat + 2, NLAT), lax.rem(lat + NLAT - 2, NLAT)
    twin = lat + 1 - 2 * lax.rem(lat, 2)
    first = 4 * lat
    barrier = pltpu.get_barrier_semaphore()

    def peer(j):
        return lax.rem(lon + j, NLON)

    def greet(j, c):
        pl.semaphore_signal(barrier, inc=1, device_id={"lon": peer(j)}, device_id_type=MESH)
        return c

    lax.fori_loop(1, NLON, greet, 0)
    for other in (up, down, up2, down2):
        pl.semaphore_signal(barrier, inc=1, device_id={"lat": other}, device_id_type=MESH)
    f_copy = pltpu.make_async_copy(f_hbm, f_ref, own_sem.at[5])
    w_copy = pltpu.make_async_copy(w_hbm, w_ref, own_sem.at[6])
    k_copy = pltpu.make_async_copy(k_hbm, k_ref, own_sem.at[0])
    f_copy.start()
    w_copy.start()
    k_copy.start()
    f_copy.wait()

    rows = [f_ref[:, r].astype(F32).reshape(48, 640) for r in range(4)]
    gap48 = jnp.zeros((48, 8), F32)
    gap8 = jnp.zeros((8, 8), F32)
    for g in range(16):
        cut = [row[:, 40 * g : 40 * g + 40] for row in rows]
        packed = jnp.concatenate([cut[0], cut[1], cut[2], gap48], axis=1)
        for e in range(2):
            last = [cut[3][24 * e + 8 * n : 24 * e + 8 * n + 8] for n in range(3)]
            both = [packed[24 * e : 24 * e + 24], jnp.concatenate(last + [gap8], axis=1)]
            m_ref[2 * g + e] = jnp.concatenate(both, axis=0).astype(BF16)
    w_copy.wait()
    odd = lax.rem(lon, 2) == 1
    four = jnp.zeros((4, 640), F32)
    for k in range(5):
        w = w_ref[k].astype(F32)
        padded = jnp.where(
            odd,
            jnp.concatenate([four, w], axis=0),
            jnp.concatenate([w, four], axis=0),
        )
        for n in range(3):
            wp_ref[3 * k + n] = padded[8 * n : 8 * n + 8].astype(BF16)
    wp_ref[15] = jnp.zeros((8, 640), BF16)

    pl.semaphore_wait(barrier, NLON + 3)

    def send_m(j):
        to = peer(j)
        return remote(m_ref.at[to], r_ref.at[lon], m_send.at[to], m_recv.at[lon], {"lon": to})

    def send_a(to):
        return remote(a_ref.at[to], ra_ref.at[lon], a_send.at[to], a_recv.at[lon], {"lon": to})

    def start_m(j, c):
        send_m(j).start()
        return c

    own_x, own_y = lon // 8, lax.rem(lon, 8)
    w_started = []

    def w_go(copy):
        copy.start()
        w_started.append(copy)

    def y_copy(d, at):
        to = 8 * own_x + lax.rem(own_y + d, 8)
        return remote(wp_ref.at[lat], g_ref.at[at], y_send.at[d], y_recv.at[d], {"lon": to})

    def x_block(d, x):
        block = g_ref.at[pl.ds(pl.multiple_of(8 * x, 8), 8)]
        to = 8 * lax.rem(own_x + d, 4) + own_y
        return remote(block, block, b_send.at[d], b_recv.at[d], {"lon": to})

    for d in range(1, 8):
        w_go(y_copy(d, lon))
    lax.fori_loop(1, NLON, start_m, 0)
    own_m = pltpu.make_async_copy(m_ref.at[lon], r_ref.at[lon], own_sem.at[1])
    own_w = pltpu.make_async_copy(wp_ref.at[lat], g_ref.at[lon], own_sem.at[2])
    own_m.start()
    own_w.start()
    q = lax.broadcasted_iota(jnp.int32, (64, 256), 0)
    lane = lax.broadcasted_iota(jnp.int32, (64, 256), 1)
    base = 32 * (q >> 3) + (q & 7)
    for o in range(4):
        spread = jnp.where(lane == base + 8 * o, 1.0, 0.0).astype(BF16)
        sp_ref[o] = spread
        sq_ref[o // 2, 64 * (o % 2) : 64 * (o % 2) + 64] = spread
    sp_ref[4] = jnp.zeros((64, 256), BF16)

    k_copy.wait()

    def pack_halo(k, c):
        for side in range(2):
            for n in range(2):
                r = 2 * (1 - side) + n
                low = low_ref[k, first + r]
                inside = (lat < NLAT - 1) if side == 0 else (lat > 0)
                halves = []
                for o in range(2):
                    t = o + 2 - n - low if side == 0 else o - 2 - n - low
                    good = (t >= 0) & (t < 3) & inside
                    block = k_ref[k, r, jnp.clip(t, 0, 2)].reshape(192, 64).astype(F32)
                    halves.append(jnp.where(good, block, 0.0))
                ku_ref[side, k, n] = jnp.concatenate(halves, axis=1).astype(BF16)
        return c

    lax.fori_loop(0, 5, pack_halo, 0)
    k_up = remote(ku_ref.at[0], kh_ref.at[0], k_send.at[0], k_recv.at[0], {"lat": up})
    k_down = remote(ku_ref.at[1], kh_ref.at[1], k_send.at[1], k_recv.at[1], {"lat": down})
    k_up.start()
    k_down.start()

    def own_rows(k, c):
        for r in range(4):
            low = low_ref[k, first + r]
            total = jnp.zeros((192, 256), F32)
            for t in range(3):
                o = r + low + t
                slot = jnp.where((o >= 0) & (o < 4), o, 4)
                total = total + jnp.dot(
                    k_ref[k, r, t].reshape(192, 64), sp_ref[slot], preferred_element_type=F32
                )
            at = 256 * (r + 2)
            rhs_ref[k, at : at + 192] = total.astype(BF16)
        for i in range(8):
            rhs_ref[k, 256 * i + 192 : 256 * i + 256] = jnp.zeros((64, 256), BF16)
        return c

    lax.fori_loop(0, 5, own_rows, 0)

    own_w.wait()
    for d in range(1, 8):
        y_copy(d, 8 * own_x + lax.rem(own_y + 8 - d, 8)).wait_recv()
    for d in range(1, 4):
        w_go(x_block(d, own_x))

    def hand_on(src):
        remote(
            r_ref.at[src], rh_ref.at[0, src], h_send.at[0], h_recv.at[0], {"lat": up}
        ).start()
        remote(
            r_ref.at[src], rh_ref.at[1, src], h_send.at[1], h_recv.at[1], {"lat": down}
        ).start()

    def take_m(j, c):
        src = lax.rem(lon + NLON - j, NLON)
        remote(
            m_ref.at[lon], r_ref.at[src], m_send.at[src], m_recv.at[src], {"lon": src}
        ).wait_recv()
        hand_on(src)
        return c

    own_m.wait()
    hand_on(lon)
    lax.fori_loop(1, NLON, take_m, 0)
    h_up = remote(r_ref, rh_ref.at[0], h_send.at[0], h_recv.at[0], {"lat": up})
    h_down = remote(r_ref, rh_ref.at[1], h_send.at[1], h_recv.at[1], {"lat": down})

    left40 = lax.broadcasted_iota(jnp.int32, (40, 128), 1) < 64

    def turn(load, first_row, wanted):
        def put(cells, u, picks):
            for p in range(3):
                t = cells[128 * p : 128 * p + 128].T
                for r, at in picks:
                    v = t[at : at + 40]
                    w = pltpu.roll(v, 64, 1)
                    x_ref[first_row + r, 6 * u + 2 * p] = jnp.where(left40, v, w)
                    x_ref[first_row + r, 6 * u + 2 * p + 1] = jnp.where(left40, w, v)

        for u in range(2):
            both = load(16 * u).astype(F32)
            picks = [(r, 40 * r) for r in wanted if r < 3]
            put(both[:, 0:24].reshape(384, 128), u, picks)
            if 3 in wanted:
                last = both[:, 24:32].reshape(128, 128)
                turned = [last, pltpu.roll(last, 88, 1), pltpu.roll(last, 48, 1)]
                cells = jnp.stack([v.reshape(16, 8, 128) for v in turned], axis=1)
                put(cells.reshape(384, 128), u, [(3, 0)])

    def gather(rows):
        for i in rows:
            row = jnp.clip(first - 2 + i, 0, 63)
            shifts = [shift_ref[j, row] + 12 for j in range(3)]

            def group(x, c, i=i, shifts=shifts):
                out = []
                for b in range(3):
                    x0, x1, x2 = [x_ref[i, lax.rem(3 * x + b + s, 12)] for s in shifts]
                    out.append(jnp.concatenate([jnp.where(left40, x0, x1), x2], axis=1))
                lhs_ref[x, :, 256 * i : 256 * i + 256] = jnp.concatenate(out, axis=0).astype(BF16)
                return c

            lax.fori_loop(0, 4, group, 0)

    turn(lambda u: r_ref[u : u + 16], 2, (0, 1, 2, 3))
    gather((2, 3, 4, 5))

    def above(n, start):
        return lax.rem(start + 2 * n, NLAT)

    def below(n, start):
        return lax.rem(start + 2 * NLAT - 2 * n, NLAT)

    started = []

    def go(copy):
        copy.start()
        started.append(copy)

    def part(n, at, half):
        return ga_ref.at[at] if n < 3 else ga_ref.at[at, pl.ds(16 * half, 16)]

    def ring_up(n):
        dst = part(n, below(n, lat), 0)
        return remote(g_ref if n == 0 else dst, dst, c_send.at[n], c_recv.at[n], {"lat": up2})

    def ring_down(n):
        dst = part(n, above(n, lat), 1)
        return remote(
            g_ref if n == 0 else dst, dst, c_send.at[4 + n], c_recv.at[4 + n], {"lat": down2}
        )

    def to_twin(slot, piece, src):
        return remote(src, ga_ref.at[piece], s_send.at[slot], s_recv.at[slot], {"lat": twin})

    def ring_step(n):
        piece = below(n, lat)
        came = part(n - 1, piece, 0)
        remote(came, came, c_send.at[n - 1], c_recv.at[n - 1], {"lat": up2}).wait_recv()
        if n < 4:
            go(ring_up(n))
            go(to_twin(n, piece, ga_ref.at[piece]))
        other = above(n, lat)
        came = part(n - 1, other, 1)
        remote(came, came, c_send.at[3 + n], c_recv.at[3 + n], {"lat": down2}).wait_recv()
        if n < 4:
            go(ring_down(n))
            go(to_twin(4 + n, other, ga_ref.at[other]))
        else:
            go(to_twin(n, piece, ga_ref.at[piece]))

    for d in range(1, 4):
        x_block(d, lax.rem(own_x + 4 - d, 4)).wait_recv()
    own_g = pltpu.make_async_copy(g_ref, ga_ref.at[lat], own_sem.at[4])
    go(ring_up(0))
    go(ring_down(0))
    own_g.start()
    go(to_twin(0, lat, g_ref))

    k_up.wait_recv()
    k_down.wait_recv()

    def halo_rows(k, c):
        for side in range(2):
            for n in range(2):
                at = 256 * (6 * side + n)
                rhs_ref[k, at : at + 192] = jnp.dot(
                    kh_ref[side, k, n], sq_ref[side], preferred_element_type=F32
                ).astype(BF16)
        return c

    lax.fori_loop(0, 5, halo_rows, 0)

    h_up.wait_recv()
    h_down.wait_recv()
    turn(lambda u: rh_ref[0, u : u + 16], -2, (2, 3))
    turn(lambda u: rh_ref[1, u : u + 16], 6, (0, 1))
    gather((0, 1, 6, 7))
    tail = jnp.zeros((40, 32), F32)
    own_a = pltpu.make_async_copy(a_ref.at[lon], ra_ref.at[lon], own_sem.at[3])
    for step in range(4):
        x = lax.rem(own_x + step, 4)

        def basis(k, c, x=x):
            acc_ref[k] = jnp.dot(lhs_ref[x], rhs_ref[k], preferred_element_type=F32)
            return c

        lax.fori_loop(0, 5, basis, 0)
        for y in range(8):
            groups = [divmod(3 * y + n, 8) for n in range(3)]
            parts = []
            for k in range(5):
                n = 0
                while n < 3:
                    beta, qg = groups[n]
                    m = n
                    while m < 3 and groups[m][0] == beta:
                        m += 1
                    parts.append(
                        acc_ref[k, 40 * beta : 40 * beta + 40, 32 * qg : 32 * (qg + m - n)]
                    )
                    n = m
            a_ref[8 * x + y] = jnp.concatenate(parts + [tail], axis=1).astype(BF16)

        def start_a(n, c, x=x):
            send_a(8 * x + lax.rem(own_y + n, 8)).start()
            return c

        lax.fori_loop(1 if step == 0 else 0, 8, start_a, 0)
        if step == 0:
            own_a.start()
        elif step == 1:
            ring_step(1)
    for n in range(2, 5):
        ring_step(n)

    for slot in range(8):
        piece = below(slot, twin) if slot < 5 else above(slot - 4, twin)
        remote(
            g_ref, ga_ref.at[piece], s_send.at[slot], s_recv.at[slot], {"lat": twin}
        ).wait_recv()
    own_g.wait()

    def order(n, c):
        k, x = n // 4, lax.rem(n, 4)
        piece = [
            ga_ref[3 * k + r, pl.ds(pl.multiple_of(8 * x, 8), 8)].astype(F32).reshape(4, 2, 8, 640)
            for r in range(3)
        ]
        even = [v[:, 0] for v in piece]
        odds = [v[:, 1] for v in piece]
        w = jnp.stack([even[0], even[1], even[2] + odds[0], odds[1], odds[2]], axis=1)
        w = jnp.concatenate([w.reshape(160, 640), jnp.zeros((96, 640), F32)], axis=0)
        wv_ref[x, pl.ds(pl.multiple_of(256 * k, 256), 256)] = w.astype(BF16)
        return c

    lax.fori_loop(0, 20, order, 0)

    for step in range(4):
        x = lax.rem(own_x + 4 - step, 4)

        def take_a(n, c, x=x):
            src = 8 * x + lax.rem(own_y + n, 8)
            remote(
                a_ref.at[lon], ra_ref.at[src], a_send.at[src], a_recv.at[src], {"lon": src}
            ).wait_recv()
            return c

        lax.fori_loop(1 if step == 0 else 0, 8, take_a, 0)
        if step == 0:
            own_a.wait()
        for e in range(2):
            parts = [ra_ref[8 * x + 2 * g + e].astype(F32) for g in range(4)]
            turned = jnp.concatenate(parts + [jnp.zeros((96, 512), F32)], axis=0).T.astype(BF16)
            for k in range(5):
                t_ref[96 * e : 96 * e + 96, 256 * k : 256 * k + 256] = turned[
                    96 * k : 96 * k + 96
                ]
        now = jnp.dot(t_ref[...], wv_ref[x], preferred_element_type=F32)
        if step == 0:
            sum_ref[...] = now
        elif step < 3:
            sum_ref[...] += now
        else:
            v = sum_ref[...] + now
            v = (v * (1.0 + lax.erf(v * 0.7071067811865476)) * 0.5).reshape(2, 3, 4, 8, 640)
            for e in range(2):
                for o in range(4):
                    o_ref[e, o] = v[e, :, o].reshape(24, 640).astype(BF16)

    def finish(j, c):
        send_a(peer(j)).wait_send()
        send_m(j).wait_send()
        return c

    lax.fori_loop(1, NLON, finish, 0)
    for copy in started + w_started + [k_up, k_down, h_up, h_down]:
        copy.wait_send()


def per_device(fields, kernel, band_low, block_shift, mix_weight):
    whole = pl.BlockSpec(memory_space=pltpu.VMEM)
    smem = pl.BlockSpec(memory_space=pltpu.SMEM)
    anywhere = pl.BlockSpec(memory_space=pl.ANY)
    shape = jax.ShapeDtypeStruct
    dma = pltpu.SemaphoreType.DMA
    vmem = pltpu.VMEM

    return pl.pallas_call(
        layer_kernel,
        out_shape=shape((2, 4, 24, 640), BF16),
        in_specs=[smem, smem, anywhere, anywhere, anywhere],
        out_specs=whole,
        scratch_shapes=[
            vmem((2, 4, 24, 640), BF16),
            vmem((5, 20, 640), BF16),
            vmem((5, 4, 3, 3, 64, 64), BF16),
            vmem((32, 32, 128), BF16),
            vmem((16, 8, 640), BF16),
            vmem((32, 32, 128), BF16),
            vmem((2, 32, 32, 128), BF16),
            vmem((32, 8, 640), BF16),
            vmem((2, 5, 2, 192, 128), BF16),
            vmem((2, 5, 2, 192, 128), BF16),
            vmem((8, 12, 40, 128), F32),
            vmem((4, 120, 2048), BF16),
            vmem((5, 2048, 256), BF16),
            vmem((5, 120, 256), F32),
            vmem((32, 40, 512), BF16),
            vmem((5, 64, 256), BF16),
            vmem((2, 128, 256), BF16),
            vmem((32, 40, 512), BF16),
            vmem((16, 32, 8, 640), BF16),
            vmem((4, 1280, 640), BF16),
            vmem((192, 1280), BF16),
            vmem((192, 640), F32),
            dma((32,)), dma((32,)), dma((8,)), dma((8,)), dma((4,)), dma((4,)),
            dma((32,)), dma((32,)), dma((2,)), dma((2,)), dma((2,)), dma((2,)),
            dma((8,)), dma((8,)), dma((8,)), dma((8,)), dma((7,)),
        ],
        compiler_params=pltpu.CompilerParams(collective_id=0, has_side_effects=True),
        name="layer",
    )(
        band_low,
        block_shift.T,
        jnp.transpose(fields, (0, 1, 3, 2)),
        mix_weight,
        kernel,
    )

def solution(mesh):
    placed = (
        P(None, "lat", None, "lon"),
        P(None, "lat", None, None, None, None),
        P(),
        P(),
        P(None, "lon", None),
    )
    return jax.shard_map(
        per_device,
        mesh=mesh,
        in_specs=placed,
        out_specs=P(None, "lat", "lon", None),
        check_vma=False,
    )
```

```python
import functools

import jax
import jax.numpy as jnp
from jax import lax
from jax.experimental import pallas as pl
from jax.experimental.pallas import tpu as pltpu
from jax.sharding import PartitionSpec as P

MESH = pl.DeviceIdType.MESH
F32 = jnp.float32
BF16 = jnp.bfloat16
NLAT, NLON = 16, 32
FULL = (0, 2, 4, 6, 8, 10, 11, 12, 13, 14)


def remote(src, dst, send, recv, where):
    return pltpu.make_async_remote_copy(
        src_ref=src,
        dst_ref=dst,
        send_sem=send,
        recv_sem=recv,
        device_id=where,
        device_id_type=MESH,
    )


def layer_kernel(
    low_ref, shift_ref, f_hbm, w_hbm, k_hbm, o_ref,
    f_ref, w_ref, k_ref, m_ref, wp_ref, r_ref, rh_ref, g_ref, ku_ref, kh_ref,
    x_ref, lhs_ref, rhs_ref, acc_ref, a_ref, sp_ref, sq_ref,
    ra_ref, ga_ref, wv_ref, t_ref, sum_ref,
    m_send, m_recv, y_send, y_recv, b_send, b_recv, a_send, a_recv,
    h_send, h_recv, k_send, k_recv, c_send, c_recv, s_send, s_recv, own_sem,
):
    lat = lax.axis_index("lat")
    lon = lax.axis_index("lon")
    up, down = lax.rem(lat + 1, NLAT), lax.rem(lat + NLAT - 1, NLAT)
    up2, down2 = lax.rem(lat + 2, NLAT), lax.rem(lat + NLAT - 2, NLAT)
    twin = lat + 1 - 2 * lax.rem(lat, 2)
    first = 4 * lat
    barrier = pltpu.get_barrier_semaphore()

    f_copy = pltpu.make_async_copy(f_hbm, f_ref, own_sem.at[5])
    w_copy = pltpu.make_async_copy(w_hbm, w_ref, own_sem.at[6])
    k_copy = pltpu.make_async_copy(k_hbm, k_ref, own_sem.at[0])
    f_copy.start()
    w_copy.start()
    k_copy.start()

    def peer(j):
        return lax.rem(lon + j, NLON)

    def greet(j, c):
        pl.semaphore_signal(barrier, inc=1, device_id={"lon": peer(j)}, device_id_type=MESH)
        return c

    lax.fori_loop(1, NLON, greet, 0)
    for other in (up, down, up2, down2):
        pl.semaphore_signal(barrier, inc=1, device_id={"lat": other}, device_id_type=MESH)
    f_copy.wait()

    rows = [f_ref[:, r].astype(F32).reshape(48, 640) for r in range(4)]
    gap48 = jnp.zeros((48, 8), F32)
    gap8 = jnp.zeros((8, 8), F32)
    for g in range(16):
        cut = [row[:, 40 * g : 40 * g + 40] for row in rows]
        packed = jnp.concatenate([cut[0], cut[1], cut[2], gap48], axis=1)
        for e in range(2):
            last = [cut[3][24 * e + 8 * n : 24 * e + 8 * n + 8] for n in range(3)]
            both = [packed[24 * e : 24 * e + 24], jnp.concatenate(last + [gap8], axis=1)]
            m_ref[2 * g + e] = jnp.concatenate(both, axis=0).astype(BF16)
    w_copy.wait()
    odd = lax.rem(lon, 2) == 1
    four = jnp.zeros((4, 640), F32)
    for k in range(5):
        w = w_ref[k].astype(F32)
        padded = jnp.where(
            odd,
            jnp.concatenate([four, w], axis=0),
            jnp.concatenate([w, four], axis=0),
        )
        groups = [padded[8 * n : 8 * n + 8] for n in range(3)]
        wp_ref[FULL[2 * k]] = jnp.where(odd, groups[1], groups[0]).astype(BF16)
        wp_ref[FULL[2 * k + 1]] = jnp.where(odd, groups[2], groups[1]).astype(BF16)
        wp_ref[2 * k + 1] = jnp.where(odd, groups[0], groups[2]).astype(BF16)
    wp_ref[15] = jnp.zeros((8, 640), BF16)

    pl.semaphore_wait(barrier, NLON + 3)

    def send_m(j):
        to = peer(j)
        return remote(m_ref.at[to], r_ref.at[lon], m_send.at[0], m_recv.at[lon], {"lon": to})

    def send_a(to, step):
        return remote(a_ref.at[to], ra_ref.at[lon], a_send.at[0], a_recv.at[step], {"lon": to})

    def start_m(j, c):
        send_m(j).start()
        return c

    own_x, own_y = lon // 8, lax.rem(lon, 8)
    w_started = []

    def w_go(copy):
        copy.start()
        w_started.append(copy)

    def y_copy(d, at):
        to = 8 * own_x + lax.rem(own_y + d, 8)
        slot = g_ref.at[lax.rem(at, 2), at // 2]
        return remote(wp_ref.at[lat], slot, y_send.at[d], y_recv.at[d], {"lon": to})

    def x_block(d, x):
        block = g_ref.at[:, pl.ds(4 * x, 4)]
        to = 8 * lax.rem(own_x + d, 4) + own_y
        return remote(block, block, b_send.at[d], b_recv.at[d], {"lon": to})

    for d in range(1, 8):
        w_go(y_copy(d, lon))
    lax.fori_loop(1, NLON, start_m, 0)
    own_m = pltpu.make_async_copy(m_ref.at[lon], r_ref.at[lon], own_sem.at[1])
    own_w = pltpu.make_async_copy(
        wp_ref.at[lat], g_ref.at[lax.rem(lon, 2), lon // 2], own_sem.at[2]
    )
    own_m.start()
    own_w.start()
    q = lax.broadcasted_iota(jnp.int32, (64, 256), 0)
    lane = lax.broadcasted_iota(jnp.int32, (64, 256), 1)
    base = 32 * (q >> 3) + (q & 7)
    for o in range(4):
        spread = jnp.where(lane == base + 8 * o, 1.0, 0.0).astype(BF16)
        sp_ref[o] = spread
        sq_ref[o // 2, 64 * (o % 2) : 64 * (o % 2) + 64] = spread
    sp_ref[4] = jnp.zeros((64, 256), BF16)

    k_copy.wait()

    def pack_halo(k, c):
        for side in range(2):
            for n in range(2):
                r = 2 * (1 - side) + n
                low = low_ref[k, first + r]
                inside = (lat < NLAT - 1) if side == 0 else (lat > 0)
                halves = []
                for o in range(2):
                    t = o + 2 - n - low if side == 0 else o - 2 - n - low
                    good = (t >= 0) & (t < 3) & inside
                    block = k_ref[k, r, jnp.clip(t, 0, 2)].reshape(192, 64).astype(F32)
                    halves.append(jnp.where(good, block, 0.0))
                ku_ref[side, k, n] = jnp.concatenate(halves, axis=1).astype(BF16)
        return c

    lax.fori_loop(0, 5, pack_halo, 0)
    k_up = remote(ku_ref.at[0], kh_ref.at[0], k_send.at[0], k_recv.at[0], {"lat": up})
    k_down = remote(ku_ref.at[1], kh_ref.at[1], k_send.at[1], k_recv.at[1], {"lat": down})
    k_up.start()
    k_down.start()

    def own_rows(k, c):
        for r in range(4):
            low = low_ref[k, first + r]
            total = jnp.zeros((192, 256), F32)
            for t in range(3):
                o = r + low + t
                slot = jnp.where((o >= 0) & (o < 4), o, 4)
                total = total + jnp.dot(
                    k_ref[k, r, t].reshape(192, 64), sp_ref[slot], preferred_element_type=F32
                )
            at = 256 * (r + 2)
            rhs_ref[k, at : at + 192] = total.astype(BF16)
        for i in range(8):
            rhs_ref[k, 256 * i + 192 : 256 * i + 256] = jnp.zeros((64, 256), BF16)
        return c

    lax.fori_loop(0, 5, own_rows, 0)

    own_w.wait()
    for d in range(1, 8):
        y_copy(d, 8 * own_x + lax.rem(own_y + 8 - d, 8)).wait_recv()
    for d in range(1, 4):
        w_go(x_block(d, own_x))

    def hand_on(src):
        remote(
            r_ref.at[src], rh_ref.at[0, src], h_send.at[0], h_recv.at[0], {"lat": up}
        ).start()
        remote(
            r_ref.at[src], rh_ref.at[1, src], h_send.at[1], h_recv.at[1], {"lat": down}
        ).start()

    def take_m(j, c):
        src = lax.rem(lon + NLON - j, NLON)
        remote(
            m_ref.at[lon], r_ref.at[src], m_send.at[0], m_recv.at[src], {"lon": src}
        ).wait_recv()
        hand_on(src)
        return c

    own_m.wait()
    hand_on(lon)
    lax.fori_loop(1, NLON, take_m, 0)
    h_up = remote(r_ref, rh_ref.at[0], h_send.at[0], h_recv.at[0], {"lat": up})
    h_down = remote(r_ref, rh_ref.at[1], h_send.at[1], h_recv.at[1], {"lat": down})

    left40 = lax.broadcasted_iota(jnp.int32, (40, 128), 1) < 64

    def turn(load, first_row, wanted):
        def put(cells, u, picks):
            for p in range(3):
                t = cells[128 * p : 128 * p + 128].T
                for r, at in picks:
                    v = t[at : at + 40]
                    w = pltpu.roll(v, 64, 1)
                    x_ref[first_row + r, 6 * u + 2 * p] = jnp.where(left40, v, w)
                    x_ref[first_row + r, 6 * u + 2 * p + 1] = jnp.where(left40, w, v)

        for u in range(2):
            both = load(16 * u).astype(F32)
            picks = [(r, 40 * r) for r in wanted if r < 3]
            put(both[:, 0:24].reshape(384, 128), u, picks)
            if 3 in wanted:
                last = both[:, 24:32].reshape(128, 128)
                turned = [last, pltpu.roll(last, 88, 1), pltpu.roll(last, 48, 1)]
                cells = jnp.stack([v.reshape(16, 8, 128) for v in turned], axis=1)
                put(cells.reshape(384, 128), u, [(3, 0)])

    def gather(rows):
        for i in rows:
            row = jnp.clip(first - 2 + i, 0, 63)
            shifts = [shift_ref[j, row] + 12 for j in range(3)]

            def group(x, c, i=i, shifts=shifts):
                out = []
                for b in range(3):
                    x0, x1, x2 = [x_ref[i, lax.rem(3 * x + b + s, 12)] for s in shifts]
                    out.append(jnp.concatenate([jnp.where(left40, x0, x1), x2], axis=1))
                lhs_ref[x, :, 256 * i : 256 * i + 256] = jnp.concatenate(out, axis=0).astype(BF16)
                return c

            lax.fori_loop(0, 4, group, 0)

    turn(lambda u: r_ref[u : u + 16], 2, (0, 1, 2, 3))
    gather((2, 3, 4, 5))

    def above(n, start):
        return lax.rem(start + 2 * n, NLAT)

    def below(n, start):
        return lax.rem(start + 2 * NLAT - 2 * n, NLAT)

    def exists(at, part):
        if part == 0:
            return at < NLAT - 1
        return (lax.rem(at, 2) == 0) | (at == 11) | (at == 13)

    started = []

    def go(at, part, make):
        make().start()
        started.append((at, part, make))

    def ring(way, n, part):
        place = ga_ref.at[(below, above)[way](n, lat), part]
        slot = 8 * way + 2 * n + part
        to = {"lat": (up2, down2)[way]}
        return remote(place, place, c_send.at[slot], c_recv.at[slot], to)

    def to_twin(slot, at, part):
        place = ga_ref.at[at, part]
        n = 2 * slot + part
        return remote(place, place, s_send.at[n], s_recv.at[n], {"lat": twin})

    def ring_step(n):
        for way in range(2):
            for part in range(2):
                if n == 4 and part != way:
                    continue
                at = (below, above)[way](n, lat)

                @pl.when(exists(at, part))
                def _():
                    place = ga_ref.at[at, part]
                    slot = 8 * way + 2 * (n - 1) + part
                    remote(
                        place, place, c_send.at[slot], c_recv.at[slot], {"lat": (up2, down2)[way]}
                    ).wait_recv()
                    if n < 3 or (n == 3 and part == way):
                        go(at, part, functools.partial(ring, way, n, part))
                    spot = n if way == 0 or n == 4 else 4 + n
                    go(at, part, functools.partial(to_twin, spot, at, part))

    for d in range(1, 4):
        x_block(d, lax.rem(own_x + 4 - d, 4)).wait_recv()
    whole = exists(lat, 1)
    even, odds = g_ref[0].astype(F32), g_ref[1]
    ga_ref[lat, 0] = jnp.where(whole, even, even + odds.astype(F32)).astype(BF16)
    ga_ref[lat, 1] = odds
    for part in range(2):

        @pl.when(exists(lat, part))
        def _():
            for way in range(2):
                go(lat, part, functools.partial(ring, way, 0, part))
            go(lat, part, functools.partial(to_twin, 0, lat, part))


    k_up.wait_recv()
    k_down.wait_recv()

    def halo_rows(k, c):
        for side in range(2):
            for n in range(2):
                at = 256 * (6 * side + n)
                rhs_ref[k, at : at + 192] = jnp.dot(
                    kh_ref[side, k, n], sq_ref[side], preferred_element_type=F32
                ).astype(BF16)
        return c

    lax.fori_loop(0, 5, halo_rows, 0)

    h_up.wait_recv()
    h_down.wait_recv()
    turn(lambda u: rh_ref[0, u : u + 16], -2, (2, 3))
    turn(lambda u: rh_ref[1, u : u + 16], 6, (0, 1))
    gather((0, 1, 6, 7))
    tail = jnp.zeros((40, 32), F32)
    own_a = pltpu.make_async_copy(a_ref.at[lon], ra_ref.at[lon], own_sem.at[3])
    for step in range(4):
        x = lax.rem(own_x + step, 4)

        def basis(k, c, x=x):
            acc_ref[k] = jnp.dot(lhs_ref[x], rhs_ref[k], preferred_element_type=F32)
            return c

        lax.fori_loop(0, 5, basis, 0)
        for y in range(8):
            groups = [divmod(3 * y + n, 8) for n in range(3)]
            parts = []
            for k in range(5):
                n = 0
                while n < 3:
                    beta, qg = groups[n]
                    m = n
                    while m < 3 and groups[m][0] == beta:
                        m += 1
                    parts.append(
                        acc_ref[k, 40 * beta : 40 * beta + 40, 32 * qg : 32 * (qg + m - n)]
                    )
                    n = m
            a_ref[8 * x + y] = jnp.concatenate(parts + [tail], axis=1).astype(BF16)

        def start_a(n, c, x=x, step=step):
            send_a(8 * x + lax.rem(own_y + n, 8), step).start()
            return c

        lax.fori_loop(1 if step == 0 else 0, 8, start_a, 0)
        if step == 0:
            own_a.start()
        elif step == 1:
            ring_step(1)
    for n in range(2, 5):
        ring_step(n)

    for slot in range(8):
        at = below(slot, twin) if slot < 5 else above(slot - 4, twin)
        for part in range(2):

            @pl.when(exists(at, part))
            def _():
                to_twin(slot, at, part).wait_recv()

    for k in range(5):

        def order(x, c, k=k):
            def cut(at, part):
                return ga_ref[at, part, pl.ds(4 * x, 4)].astype(F32)

            one, two = FULL[2 * k], FULL[2 * k + 1]
            w = jnp.stack(
                [cut(one, 0), cut(two, 0), cut(2 * k + 1, 0), cut(one, 1), cut(two, 1)], axis=1
            )
            w = jnp.concatenate([w.reshape(160, 640), jnp.zeros((96, 640), F32)], axis=0)
            wv_ref[x, 256 * k : 256 * k + 256] = w.astype(BF16)
            return c

        lax.fori_loop(0, 4, order, 0)

    for step in range(4):
        x = lax.rem(own_x + 4 - step, 4)

        count = pl.ds(0, 7 if step == 0 else 8)
        remote(
            a_ref.at[count], ra_ref.at[count], a_send.at[0], a_recv.at[step], {"lon": peer(1)}
        ).wait_recv()
        if step == 0:
            own_a.wait()
        for e in range(2):
            parts = [ra_ref[8 * x + 2 * g + e].astype(F32) for g in range(4)]
            turned = jnp.concatenate(parts + [jnp.zeros((96, 512), F32)], axis=0).T.astype(BF16)
            for k in range(5):
                t_ref[96 * e : 96 * e + 96, 256 * k : 256 * k + 256] = turned[
                    96 * k : 96 * k + 96
                ]
        now = jnp.dot(t_ref[...], wv_ref[x], preferred_element_type=F32)
        if step == 0:
            sum_ref[...] = now
        elif step < 3:
            sum_ref[...] += now
        else:
            v = sum_ref[...] + now
            v = (v * (1.0 + lax.erf(v * 0.7071067811865476)) * 0.5).reshape(2, 3, 4, 8, 640)
            for e in range(2):
                for o in range(4):
                    o_ref[e, o] = v[e, :, o].reshape(24, 640).astype(BF16)

    others = pl.ds(0, NLON - 1)
    to = {"lon": peer(1)}
    remote(m_ref.at[others], r_ref.at[others], m_send.at[0], m_recv.at[0], to).wait_send()
    remote(a_ref.at[others], ra_ref.at[others], a_send.at[0], a_recv.at[0], to).wait_send()
    for copy in w_started + [k_up, k_down, h_up, h_down]:
        copy.wait_send()
    for at, part, make in started:

        @pl.when(exists(at, part))
        def _():
            make().wait_send()


def per_device(fields, kernel, band_low, block_shift, mix_weight):
    whole = pl.BlockSpec(memory_space=pltpu.VMEM)
    smem = pl.BlockSpec(memory_space=pltpu.SMEM)
    anywhere = pl.BlockSpec(memory_space=pl.ANY)
    shape = jax.ShapeDtypeStruct
    dma = pltpu.SemaphoreType.DMA
    vmem = pltpu.VMEM

    return pl.pallas_call(
        layer_kernel,
        out_shape=shape((2, 4, 24, 640), BF16),
        in_specs=[smem, smem, anywhere, anywhere, anywhere],
        out_specs=whole,
        scratch_shapes=[
            vmem((2, 4, 24, 640), BF16),
            vmem((5, 20, 640), BF16),
            vmem((5, 4, 3, 3, 64, 64), BF16),
            vmem((32, 32, 128), BF16),
            vmem((16, 8, 640), BF16),
            vmem((32, 32, 128), BF16),
            vmem((2, 32, 32, 128), BF16),
            vmem((2, 16, 8, 640), BF16),
            vmem((2, 5, 2, 192, 128), BF16),
            vmem((2, 5, 2, 192, 128), BF16),
            vmem((8, 12, 40, 128), F32),
            vmem((4, 120, 2048), BF16),
            vmem((5, 2048, 256), BF16),
            vmem((5, 120, 256), F32),
            vmem((32, 40, 512), BF16),
            vmem((5, 64, 256), BF16),
            vmem((2, 128, 256), BF16),
            vmem((32, 40, 512), BF16),
            vmem((16, 2, 16, 8, 640), BF16),
            vmem((4, 1280, 640), BF16),
            vmem((192, 1280), BF16),
            vmem((192, 640), F32),
            dma((1,)), dma((32,)), dma((8,)), dma((8,)), dma((4,)), dma((4,)),
            dma((1,)), dma((4,)), dma((2,)), dma((2,)), dma((2,)), dma((2,)),
            dma((16,)), dma((16,)), dma((16,)), dma((16,)), dma((7,)),
        ],
        compiler_params=pltpu.CompilerParams(collective_id=0, has_side_effects=True),
        name="layer",
    )(
        band_low,
        block_shift.T,
        jnp.transpose(fields, (0, 1, 3, 2)),
        mix_weight,
        kernel,
    )

def solution(mesh):
    placed = (
        P(None, "lat", None, "lon"),
        P(None, "lat", None, None, None, None),
        P(),
        P(),
        P(None, "lon", None),
    )
    return jax.shard_map(
        per_device,
        mesh=mesh,
        in_specs=placed,
        out_specs=P(None, "lat", "lon", None),
        check_vma=False,
    )
```

```python
import functools

import jax
import jax.numpy as jnp
from jax import lax
from jax.experimental import pallas as pl
from jax.experimental.pallas import tpu as pltpu
from jax.sharding import PartitionSpec as P

MESH = pl.DeviceIdType.MESH
F32 = jnp.float32
BF16 = jnp.bfloat16
NLAT, NLON = 16, 32
FULL = (0, 2, 4, 6, 8, 10, 11, 12, 13, 14)


def remote(src, dst, send, recv, where):
    return pltpu.make_async_remote_copy(
        src_ref=src,
        dst_ref=dst,
        send_sem=send,
        recv_sem=recv,
        device_id=where,
        device_id_type=MESH,
    )


def layer_kernel(
    low_hbm, shift_hbm, f_hbm, w_hbm, k_hbm, o_ref,
    low_ref, shift_ref, f_ref, w_ref, k_ref, m_ref, wp_ref, r_ref, rh_ref, g_ref, ku_ref, kh_ref,
    x_ref, lhs_ref, rhs_ref, acc_ref, a_ref, sp_ref, sq_ref,
    ra_ref, ga_ref, wv_ref, t_ref, sum_ref,
    m_send, m_recv, y_send, y_recv, b_send, b_recv, a_send, a_recv,
    h_send, h_recv, k_send, k_recv, c_send, c_recv, s_send, s_recv, own_sem,
):
    lat = lax.axis_index("lat")
    lon = lax.axis_index("lon")
    up, down = lax.rem(lat + 1, NLAT), lax.rem(lat + NLAT - 1, NLAT)
    up2, down2 = lax.rem(lat + 2, NLAT), lax.rem(lat + NLAT - 2, NLAT)
    twin = lat + 1 - 2 * lax.rem(lat, 2)
    first = 4 * lat
    barrier = pltpu.get_barrier_semaphore()

    f_copy = pltpu.make_async_copy(f_hbm, f_ref, own_sem.at[5])
    w_copy = pltpu.make_async_copy(w_hbm, w_ref, own_sem.at[6])
    k_copy = pltpu.make_async_copy(k_hbm, k_ref, own_sem.at[0])
    low_copy = pltpu.make_async_copy(low_hbm, low_ref, own_sem.at[4])
    shift_copy = pltpu.make_async_copy(shift_hbm, shift_ref, own_sem.at[7])
    f_copy.start()
    low_copy.start()
    shift_copy.start()
    w_copy.start()
    k_copy.start()

    def peer(j):
        return lax.rem(lon + j, NLON)

    def greet(j, c):
        pl.semaphore_signal(barrier, inc=1, device_id={"lon": peer(j)}, device_id_type=MESH)
        return c

    lax.fori_loop(1, NLON, greet, 0)
    for other in (up, down, up2, down2):
        pl.semaphore_signal(barrier, inc=1, device_id={"lat": other}, device_id_type=MESH)
    f_copy.wait()

    rows = [f_ref[:, r].astype(F32).reshape(48, 640) for r in range(4)]
    gap48 = jnp.zeros((48, 8), F32)
    gap8 = jnp.zeros((8, 8), F32)
    for g in range(16):
        cut = [row[:, 40 * g : 40 * g + 40] for row in rows]
        packed = jnp.concatenate([cut[0], cut[1], cut[2], gap48], axis=1)
        for e in range(2):
            last = [cut[3][24 * e + 8 * n : 24 * e + 8 * n + 8] for n in range(3)]
            both = [packed[24 * e : 24 * e + 24], jnp.concatenate(last + [gap8], axis=1)]
            m_ref[2 * g + e] = jnp.concatenate(both, axis=0).astype(BF16)
    w_copy.wait()
    odd = lax.rem(lon, 2) == 1
    four = jnp.zeros((4, 640), F32)
    for k in range(5):
        w = w_ref[k].astype(F32)
        padded = jnp.where(
            odd,
            jnp.concatenate([four, w], axis=0),
            jnp.concatenate([w, four], axis=0),
        )
        groups = [padded[8 * n : 8 * n + 8] for n in range(3)]
        wp_ref[FULL[2 * k]] = jnp.where(odd, groups[1], groups[0]).astype(BF16)
        wp_ref[FULL[2 * k + 1]] = jnp.where(odd, groups[2], groups[1]).astype(BF16)
        wp_ref[2 * k + 1] = jnp.where(odd, groups[0], groups[2]).astype(BF16)
    wp_ref[15] = jnp.zeros((8, 640), BF16)

    pl.semaphore_wait(barrier, NLON + 3)

    def send_m(j):
        to = peer(j)
        return remote(m_ref.at[to], r_ref.at[lon], m_send.at[0], m_recv.at[lon], {"lon": to})

    def send_a(to, step):
        return remote(a_ref.at[to], ra_ref.at[lon], a_send.at[0], a_recv.at[step], {"lon": to})

    def start_m(j, c):
        send_m(j).start()
        return c

    own_x, own_y = lon // 8, lax.rem(lon, 8)
    w_started = []

    def w_go(copy):
        copy.start()
        w_started.append(copy)

    def y_copy(d, at):
        to = 8 * own_x + lax.rem(own_y + d, 8)
        slot = g_ref.at[lax.rem(at, 2), at // 2]
        return remote(wp_ref.at[lat], slot, y_send.at[d], y_recv.at[d], {"lon": to})

    def x_block(d, x):
        block = g_ref.at[:, pl.ds(4 * x, 4)]
        to = 8 * lax.rem(own_x + d, 4) + own_y
        return remote(block, block, b_send.at[d], b_recv.at[d], {"lon": to})

    lax.fori_loop(1, NLON, start_m, 0)
    for d in range(1, 8):
        w_go(y_copy(d, lon))
    own_m = pltpu.make_async_copy(m_ref.at[lon], r_ref.at[lon], own_sem.at[1])
    own_w = pltpu.make_async_copy(
        wp_ref.at[lat], g_ref.at[lax.rem(lon, 2), lon // 2], own_sem.at[2]
    )
    own_m.start()
    own_w.start()
    q = lax.broadcasted_iota(jnp.int32, (64, 256), 0)
    lane = lax.broadcasted_iota(jnp.int32, (64, 256), 1)
    base = 32 * (q >> 3) + (q & 7)
    for o in range(4):
        spread = jnp.where(lane == base + 8 * o, 1.0, 0.0).astype(BF16)
        sp_ref[o] = spread
        sq_ref[o // 2, 64 * (o % 2) : 64 * (o % 2) + 64] = spread
    sp_ref[4] = jnp.zeros((64, 256), BF16)

    k_copy.wait()
    low_copy.wait()
    shift_copy.wait()

    def pack_halo(k, c):
        for side in range(2):
            for n in range(2):
                r = 2 * (1 - side) + n
                low = low_ref[k, first + r]
                inside = (lat < NLAT - 1) if side == 0 else (lat > 0)
                halves = []
                for o in range(2):
                    t = o + 2 - n - low if side == 0 else o - 2 - n - low
                    good = (t >= 0) & (t < 3) & inside
                    block = k_ref[k, r, jnp.clip(t, 0, 2)].reshape(192, 64).astype(F32)
                    halves.append(jnp.where(good, block, 0.0))
                ku_ref[side, k, n] = jnp.concatenate(halves, axis=1).astype(BF16)
        return c

    lax.fori_loop(0, 5, pack_halo, 0)
    k_up = remote(ku_ref.at[0], kh_ref.at[0], k_send.at[0], k_recv.at[0], {"lat": up})
    k_down = remote(ku_ref.at[1], kh_ref.at[1], k_send.at[1], k_recv.at[1], {"lat": down})
    k_up.start()
    k_down.start()

    def own_rows(k, c):
        for r in range(4):
            low = low_ref[k, first + r]
            total = jnp.zeros((192, 256), F32)
            for t in range(3):
                o = r + low + t
                slot = jnp.where((o >= 0) & (o < 4), o, 4)
                total = total + jnp.dot(
                    k_ref[k, r, t].reshape(192, 64), sp_ref[slot], preferred_element_type=F32
                )
            at = 256 * (r + 2)
            rhs_ref[k, at : at + 192] = total.astype(BF16)
        for i in range(8):
            rhs_ref[k, 256 * i + 192 : 256 * i + 256] = jnp.zeros((64, 256), BF16)
        return c

    lax.fori_loop(0, 5, own_rows, 0)


    def hand_on(src):
        remote(
            r_ref.at[src], rh_ref.at[0, src], h_send.at[0], h_recv.at[0], {"lat": up}
        ).start()
        remote(
            r_ref.at[src], rh_ref.at[1, src], h_send.at[1], h_recv.at[1], {"lat": down}
        ).start()

    def take_m(j, c):
        src = lax.rem(lon + NLON - j, NLON)
        remote(
            m_ref.at[lon], r_ref.at[src], m_send.at[0], m_recv.at[src], {"lon": src}
        ).wait_recv()
        hand_on(src)
        return c

    own_m.wait()
    hand_on(lon)
    lax.fori_loop(1, NLON, take_m, 0)
    h_up = remote(r_ref, rh_ref.at[0], h_send.at[0], h_recv.at[0], {"lat": up})
    h_down = remote(r_ref, rh_ref.at[1], h_send.at[1], h_recv.at[1], {"lat": down})

    left40 = lax.broadcasted_iota(jnp.int32, (40, 128), 1) < 64

    def turn(load, first_row, wanted):
        def put(cells, u, picks):
            for p in range(3):
                t = cells[128 * p : 128 * p + 128].T
                for r, at in picks:
                    v = t[at : at + 40]
                    w = pltpu.roll(v, 64, 1)
                    x_ref[first_row + r, 6 * u + 2 * p] = jnp.where(left40, v, w)
                    x_ref[first_row + r, 6 * u + 2 * p + 1] = jnp.where(left40, w, v)

        for u in range(2):
            both = load(16 * u).astype(F32)
            picks = [(r, 40 * r) for r in wanted if r < 3]
            put(both[:, 0:24].reshape(384, 128), u, picks)
            if 3 in wanted:
                last = both[:, 24:32].reshape(128, 128)
                turned = [last, pltpu.roll(last, 88, 1), pltpu.roll(last, 48, 1)]
                cells = jnp.stack([v.reshape(16, 8, 128) for v in turned], axis=1)
                put(cells.reshape(384, 128), u, [(3, 0)])

    def gather(rows):
        for i in rows:
            row = jnp.clip(first - 2 + i, 0, 63)
            shifts = [shift_ref[j, row] + 12 for j in range(3)]

            def group(x, c, i=i, shifts=shifts):
                out = []
                for b in range(3):
                    x0, x1, x2 = [x_ref[i, lax.rem(3 * x + b + s, 12)] for s in shifts]
                    out.append(jnp.concatenate([jnp.where(left40, x0, x1), x2], axis=1))
                lhs_ref[x, :, 256 * i : 256 * i + 256] = jnp.concatenate(out, axis=0).astype(BF16)
                return c

            lax.fori_loop(0, 4, group, 0)

    turn(lambda u: r_ref[u : u + 16], 2, (0, 1, 2, 3))
    own_w.wait()
    for d in range(1, 8):
        y_copy(d, 8 * own_x + lax.rem(own_y + 8 - d, 8)).wait_recv()
    for d in range(1, 4):
        w_go(x_block(d, own_x))
    gather((2, 3, 4, 5))

    def above(n, start):
        return lax.rem(start + 2 * n, NLAT)

    def below(n, start):
        return lax.rem(start + 2 * NLAT - 2 * n, NLAT)

    def exists(at, part):
        if part == 0:
            return at < NLAT - 1
        return (lax.rem(at, 2) == 0) | (at == 11) | (at == 13)

    started = []

    def go(at, part, make):
        make().start()
        started.append((at, part, make))

    def ring(way, n, part):
        place = ga_ref.at[(below, above)[way](n, lat), part]
        slot = 8 * way + 2 * n + part
        to = {"lat": (up2, down2)[way]}
        return remote(place, place, c_send.at[slot], c_recv.at[slot], to)

    def to_twin(slot, at, part):
        place = ga_ref.at[at, part]
        n = 2 * slot + part
        return remote(place, place, s_send.at[n], s_recv.at[n], {"lat": twin})

    def ring_step(n):
        for way in range(2):
            for part in range(2):
                if n == 4 and part != way:
                    continue
                at = (below, above)[way](n, lat)

                @pl.when(exists(at, part))
                def _():
                    place = ga_ref.at[at, part]
                    slot = 8 * way + 2 * (n - 1) + part
                    remote(
                        place, place, c_send.at[slot], c_recv.at[slot], {"lat": (up2, down2)[way]}
                    ).wait_recv()
                    if n < 3 or (n == 3 and part == way):
                        go(at, part, functools.partial(ring, way, n, part))
                    spot = n if way == 0 or n == 4 else 4 + n
                    go(at, part, functools.partial(to_twin, spot, at, part))

    k_up.wait_recv()
    k_down.wait_recv()

    def halo_rows(k, c):
        for side in range(2):
            for n in range(2):
                at = 256 * (6 * side + n)
                rhs_ref[k, at : at + 192] = jnp.dot(
                    kh_ref[side, k, n], sq_ref[side], preferred_element_type=F32
                ).astype(BF16)
        return c

    lax.fori_loop(0, 5, halo_rows, 0)

    h_up.wait_recv()
    h_down.wait_recv()
    for d in range(1, 4):
        x_block(d, lax.rem(own_x + 4 - d, 4)).wait_recv()
    whole = exists(lat, 1)
    even, odds = g_ref[0].astype(F32), g_ref[1]
    ga_ref[lat, 0] = jnp.where(whole, even, even + odds.astype(F32)).astype(BF16)
    ga_ref[lat, 1] = odds
    for part in range(2):

        @pl.when(exists(lat, part))
        def _():
            for way in range(2):
                go(lat, part, functools.partial(ring, way, 0, part))
            go(lat, part, functools.partial(to_twin, 0, lat, part))


    turn(lambda u: rh_ref[0, u : u + 16], -2, (2, 3))
    turn(lambda u: rh_ref[1, u : u + 16], 6, (0, 1))
    gather((0, 1, 6, 7))
    tail = jnp.zeros((40, 32), F32)
    own_a = pltpu.make_async_copy(a_ref.at[lon], ra_ref.at[lon], own_sem.at[3])
    for step in range(4):
        x = lax.rem(own_x + step, 4)

        def basis(k, c, x=x):
            acc_ref[k] = jnp.dot(lhs_ref[x], rhs_ref[k], preferred_element_type=F32)
            return c

        lax.fori_loop(0, 5, basis, 0)
        for y in range(8):
            groups = [divmod(3 * y + n, 8) for n in range(3)]
            parts = []
            for k in range(5):
                n = 0
                while n < 3:
                    beta, qg = groups[n]
                    m = n
                    while m < 3 and groups[m][0] == beta:
                        m += 1
                    parts.append(
                        acc_ref[k, 40 * beta : 40 * beta + 40, 32 * qg : 32 * (qg + m - n)]
                    )
                    n = m
            a_ref[8 * x + y] = jnp.concatenate(parts + [tail], axis=1).astype(BF16)

        def start_a(n, c, x=x, step=step):
            send_a(8 * x + lax.rem(own_y + n, 8), step).start()
            return c

        lax.fori_loop(1 if step == 0 else 0, 8, start_a, 0)
        if step == 0:
            own_a.start()
        elif step == 1:
            ring_step(1)
    for n in range(2, 5):
        ring_step(n)

    for slot in range(8):
        at = below(slot, twin) if slot < 5 else above(slot - 4, twin)
        for part in range(2):

            @pl.when(exists(at, part))
            def _():
                to_twin(slot, at, part).wait_recv()

    for k in range(5):

        def order(x, c, k=k):
            def cut(at, part):
                return ga_ref[at, part, pl.ds(4 * x, 4)].astype(F32)

            one, two = FULL[2 * k], FULL[2 * k + 1]
            w = jnp.stack(
                [cut(one, 0), cut(two, 0), cut(2 * k + 1, 0), cut(one, 1), cut(two, 1)], axis=1
            )
            w = jnp.concatenate([w.reshape(160, 640), jnp.zeros((96, 640), F32)], axis=0)
            wv_ref[x, 256 * k : 256 * k + 256] = w.astype(BF16)
            return c

        lax.fori_loop(0, 4, order, 0)

    for step in range(4):
        x = lax.rem(own_x + 4 - step, 4)

        count = pl.ds(0, 7 if step == 0 else 8)
        remote(
            a_ref.at[count], ra_ref.at[count], a_send.at[0], a_recv.at[step], {"lon": peer(1)}
        ).wait_recv()
        if step == 0:
            own_a.wait()
        for e in range(2):
            parts = [ra_ref[8 * x + 2 * g + e].astype(F32) for g in range(4)]
            turned = jnp.concatenate(parts + [jnp.zeros((96, 512), F32)], axis=0).T.astype(BF16)
            for k in range(5):
                t_ref[96 * e : 96 * e + 96, 256 * k : 256 * k + 256] = turned[
                    96 * k : 96 * k + 96
                ]
        now = jnp.dot(t_ref[...], wv_ref[x], preferred_element_type=F32)
        if step == 0:
            sum_ref[...] = now
        elif step < 3:
            sum_ref[...] += now
        else:
            v = sum_ref[...] + now
            v = (v * (1.0 + lax.erf(v * 0.7071067811865476)) * 0.5).reshape(2, 3, 4, 8, 640)
            for e in range(2):
                for o in range(4):
                    o_ref[e, o] = v[e, :, o].reshape(24, 640).astype(BF16)

    others = pl.ds(0, NLON - 1)
    to = {"lon": peer(1)}
    remote(m_ref.at[others], r_ref.at[others], m_send.at[0], m_recv.at[0], to).wait_send()
    remote(a_ref.at[others], ra_ref.at[others], a_send.at[0], a_recv.at[0], to).wait_send()
    for copy in w_started + [k_up, k_down, h_up, h_down]:
        copy.wait_send()
    for at, part, make in started:

        @pl.when(exists(at, part))
        def _():
            make().wait_send()


def per_device(fields, kernel, band_low, block_shift, mix_weight):
    whole = pl.BlockSpec(memory_space=pltpu.VMEM)
    anywhere = pl.BlockSpec(memory_space=pl.ANY)
    shape = jax.ShapeDtypeStruct
    dma = pltpu.SemaphoreType.DMA
    vmem = pltpu.VMEM

    return pl.pallas_call(
        layer_kernel,
        out_shape=pltpu.VMEM((2, 4, 24, 640), BF16),
        in_specs=[anywhere] * 5,
        out_specs=whole,
        scratch_shapes=[
            pltpu.SMEM((5, 64), jnp.int32),
            pltpu.SMEM((3, 64), jnp.int32),
            vmem((2, 4, 24, 640), BF16),
            vmem((5, 20, 640), BF16),
            vmem((5, 4, 3, 3, 64, 64), BF16),
            vmem((32, 32, 128), BF16),
            vmem((16, 8, 640), BF16),
            vmem((32, 32, 128), BF16),
            vmem((2, 32, 32, 128), BF16),
            vmem((2, 16, 8, 640), BF16),
            vmem((2, 5, 2, 192, 128), BF16),
            vmem((2, 5, 2, 192, 128), BF16),
            vmem((8, 12, 40, 128), F32),
            vmem((4, 120, 2048), BF16),
            vmem((5, 2048, 256), BF16),
            vmem((5, 120, 256), F32),
            vmem((32, 40, 512), BF16),
            vmem((5, 64, 256), BF16),
            vmem((2, 128, 256), BF16),
            vmem((32, 40, 512), BF16),
            vmem((16, 2, 16, 8, 640), BF16),
            vmem((4, 1280, 640), BF16),
            vmem((192, 1280), BF16),
            vmem((192, 640), F32),
            dma((1,)), dma((32,)), dma((8,)), dma((8,)), dma((4,)), dma((4,)),
            dma((1,)), dma((4,)), dma((2,)), dma((2,)), dma((2,)), dma((2,)),
            dma((16,)), dma((16,)), dma((16,)), dma((16,)), dma((8,)),
        ],
        compiler_params=pltpu.CompilerParams(collective_id=0, has_side_effects=True),
        name="layer",
    )(
        band_low,
        block_shift.T,
        jnp.transpose(fields, (0, 1, 3, 2)),
        mix_weight,
        kernel,
    )

def solution(mesh):
    placed = (
        P(None, "lat", None, "lon"),
        P(None, "lat", None, None, None, None),
        P(),
        P(),
        P(None, "lon", None),
    )
    return jax.shard_map(
        per_device,
        mesh=mesh,
        in_specs=placed,
        out_specs=P(None, "lat", "lon", None),
        check_vma=False,
    )
```

```python
import functools

import jax
import jax.numpy as jnp
from jax import lax
from jax.experimental import pallas as pl
from jax.experimental.pallas import tpu as pltpu
from jax.sharding import PartitionSpec as P

MESH = pl.DeviceIdType.MESH
F32 = jnp.float32
BF16 = jnp.bfloat16
NLAT, NLON = 16, 32
FULL = (0, 2, 4, 6, 8, 10, 11, 12, 13, 14)


def remote(src, dst, send, recv, where):
    return pltpu.make_async_remote_copy(
        src_ref=src,
        dst_ref=dst,
        send_sem=send,
        recv_sem=recv,
        device_id=where,
        device_id_type=MESH,
    )


def layer_kernel(
    low_hbm, shift_hbm, f_hbm, w_hbm, k_hbm, o_ref,
    low_ref, shift_ref, f_ref, w_ref, k_ref, m_ref, wp_ref, r_ref, rh_ref, g_ref, ku_ref, kh_ref,
    x_ref, lhs_ref, rhs_ref, acc_ref, a_ref, b_ref, sp_ref, sq_ref,
    ra_ref, rb_ref, ga_ref, wv_ref, t_ref, sum_ref,
    m_send, m_recv, y_send, y_recv, b_send, b_recv, a_send, a_recv,
    h_send, h_recv, k_send, k_recv, c_send, c_recv, s_send, s_recv, own_sem,
):
    lat = lax.axis_index("lat")
    lon = lax.axis_index("lon")
    up, down = lax.rem(lat + 1, NLAT), lax.rem(lat + NLAT - 1, NLAT)
    up2, down2 = lax.rem(lat + 2, NLAT), lax.rem(lat + NLAT - 2, NLAT)
    twin = lat + 1 - 2 * lax.rem(lat, 2)
    first = 4 * lat
    barrier = pltpu.get_barrier_semaphore()

    f_copy = pltpu.make_async_copy(f_hbm, f_ref, own_sem.at[5])
    w_copy = pltpu.make_async_copy(w_hbm, w_ref, own_sem.at[6])
    k_copy = pltpu.make_async_copy(k_hbm, k_ref, own_sem.at[0])
    low_copy = pltpu.make_async_copy(low_hbm, low_ref, own_sem.at[4])
    shift_copy = pltpu.make_async_copy(shift_hbm, shift_ref, own_sem.at[7])
    f_copy.start()
    low_copy.start()
    shift_copy.start()
    w_copy.start()
    k_copy.start()

    def peer(j):
        return lax.rem(lon + j, NLON)

    def greet(j, c):
        pl.semaphore_signal(barrier, inc=1, device_id={"lon": peer(j)}, device_id_type=MESH)
        return c

    lax.fori_loop(1, NLON, greet, 0)
    for other in (up, down, up2, down2):
        pl.semaphore_signal(barrier, inc=1, device_id={"lat": other}, device_id_type=MESH)
    f_copy.wait()

    rows = [f_ref[:, r].astype(F32).reshape(48, 640) for r in range(4)]
    gap48 = jnp.zeros((48, 8), F32)
    gap8 = jnp.zeros((8, 8), F32)
    for g in range(16):
        cut = [row[:, 40 * g : 40 * g + 40] for row in rows]
        packed = jnp.concatenate([cut[0], cut[1], cut[2], gap48], axis=1)
        for e in range(2):
            last = [cut[3][24 * e + 8 * n : 24 * e + 8 * n + 8] for n in range(3)]
            both = [packed[24 * e : 24 * e + 24], jnp.concatenate(last + [gap8], axis=1)]
            m_ref[2 * g + e] = jnp.concatenate(both, axis=0).astype(BF16)
    w_copy.wait()
    odd = lax.rem(lon, 2) == 1
    four = jnp.zeros((4, 640), F32)
    for k in range(5):
        w = w_ref[k].astype(F32)
        padded = jnp.where(
            odd,
            jnp.concatenate([four, w], axis=0),
            jnp.concatenate([w, four], axis=0),
        )
        groups = [padded[8 * n : 8 * n + 8] for n in range(3)]
        wp_ref[FULL[2 * k]] = jnp.where(odd, groups[1], groups[0]).astype(BF16)
        wp_ref[FULL[2 * k + 1]] = jnp.where(odd, groups[2], groups[1]).astype(BF16)
        wp_ref[2 * k + 1] = jnp.where(odd, groups[0], groups[2]).astype(BF16)
    wp_ref[15] = jnp.zeros((8, 640), BF16)

    pl.semaphore_wait(barrier, NLON + 3)

    def send_m(j):
        to = peer(j)
        return remote(m_ref.at[to], r_ref.at[lon], m_send.at[0], m_recv.at[lon], {"lon": to})

    def send_a(to, step):
        return remote(a_ref.at[to], ra_ref.at[lon], a_send.at[0], a_recv.at[step], {"lon": to})

    def send_b(to, step):
        return remote(
            b_ref.at[to], rb_ref.at[lon], a_send.at[1], a_recv.at[4 + step], {"lon": to}
        )

    def start_m(j, c):
        send_m(j).start()
        return c

    own_x, own_y = lon // 8, lax.rem(lon, 8)
    w_started = []

    def w_go(copy):
        copy.start()
        w_started.append(copy)

    def y_copy(d, at):
        to = 8 * own_x + lax.rem(own_y + d, 8)
        slot = g_ref.at[lax.rem(at, 2), at // 2]
        return remote(wp_ref.at[lat], slot, y_send.at[d], y_recv.at[d], {"lon": to})

    def x_block(d, x):
        block = g_ref.at[:, pl.ds(4 * x, 4)]
        to = 8 * lax.rem(own_x + d, 4) + own_y
        return remote(block, block, b_send.at[d], b_recv.at[d], {"lon": to})

    lax.fori_loop(1, NLON, start_m, 0)
    for d in range(1, 8):
        w_go(y_copy(d, lon))
    own_m = pltpu.make_async_copy(m_ref.at[lon], r_ref.at[lon], own_sem.at[1])
    own_w = pltpu.make_async_copy(
        wp_ref.at[lat], g_ref.at[lax.rem(lon, 2), lon // 2], own_sem.at[2]
    )
    own_m.start()
    own_w.start()
    q = lax.broadcasted_iota(jnp.int32, (64, 256), 0)
    lane = lax.broadcasted_iota(jnp.int32, (64, 256), 1)
    base = 32 * (q >> 3) + (q & 7)
    for o in range(4):
        spread = jnp.where(lane == base + 8 * o, 1.0, 0.0).astype(BF16)
        sp_ref[o] = spread
        sq_ref[o // 2, 64 * (o % 2) : 64 * (o % 2) + 64] = spread
    sp_ref[4] = jnp.zeros((64, 256), BF16)

    k_copy.wait()
    low_copy.wait()
    shift_copy.wait()

    def pack_halo(k, c):
        for side in range(2):
            for n in range(2):
                r = 2 * (1 - side) + n
                low = low_ref[k, first + r]
                inside = (lat < NLAT - 1) if side == 0 else (lat > 0)
                halves = []
                for o in range(2):
                    t = o + 2 - n - low if side == 0 else o - 2 - n - low
                    good = (t >= 0) & (t < 3) & inside
                    block = k_ref[k, r, jnp.clip(t, 0, 2)].reshape(192, 64).astype(F32)
                    halves.append(jnp.where(good, block, 0.0))
                ku_ref[side, k, n] = jnp.concatenate(halves, axis=1).astype(BF16)
        return c

    lax.fori_loop(0, 5, pack_halo, 0)
    k_up = remote(ku_ref.at[0], kh_ref.at[0], k_send.at[0], k_recv.at[0], {"lat": up})
    k_down = remote(ku_ref.at[1], kh_ref.at[1], k_send.at[1], k_recv.at[1], {"lat": down})
    k_up.start()
    k_down.start()

    def own_rows(k, c):
        for r in range(4):
            low = low_ref[k, first + r]
            total = jnp.zeros((192, 256), F32)
            for t in range(3):
                o = r + low + t
                slot = jnp.where((o >= 0) & (o < 4), o, 4)
                total = total + jnp.dot(
                    k_ref[k, r, t].reshape(192, 64), sp_ref[slot], preferred_element_type=F32
                )
            at = 256 * (r + 2)
            rhs_ref[k, at : at + 192] = total.astype(BF16)
        for i in range(8):
            rhs_ref[k, 256 * i + 192 : 256 * i + 256] = jnp.zeros((64, 256), BF16)
        return c

    lax.fori_loop(0, 5, own_rows, 0)


    def hand_on(src):
        remote(
            r_ref.at[src], rh_ref.at[0, src], h_send.at[0], h_recv.at[0], {"lat": up}
        ).start()
        remote(
            r_ref.at[src], rh_ref.at[1, src], h_send.at[1], h_recv.at[1], {"lat": down}
        ).start()

    def take_m(j, c):
        src = lax.rem(lon + NLON - j, NLON)
        remote(
            m_ref.at[lon], r_ref.at[src], m_send.at[0], m_recv.at[src], {"lon": src}
        ).wait_recv()
        hand_on(src)
        return c

    own_m.wait()
    hand_on(lon)
    lax.fori_loop(1, NLON, take_m, 0)
    h_up = remote(r_ref, rh_ref.at[0], h_send.at[0], h_recv.at[0], {"lat": up})
    h_down = remote(r_ref, rh_ref.at[1], h_send.at[1], h_recv.at[1], {"lat": down})

    left40 = lax.broadcasted_iota(jnp.int32, (40, 128), 1) < 64

    def turn(load, first_row, wanted):
        def put(cells, u, picks):
            for p in range(3):
                t = cells[128 * p : 128 * p + 128].T
                for r, at in picks:
                    v = t[at : at + 40]
                    w = pltpu.roll(v, 64, 1)
                    x_ref[first_row + r, 6 * u + 2 * p] = jnp.where(left40, v, w)
                    x_ref[first_row + r, 6 * u + 2 * p + 1] = jnp.where(left40, w, v)

        for u in range(2):
            both = load(16 * u).astype(F32)
            picks = [(r, 40 * r) for r in wanted if r < 3]
            put(both[:, 0:24].reshape(384, 128), u, picks)
            if 3 in wanted:
                last = both[:, 24:32].reshape(128, 128)
                turned = [last, pltpu.roll(last, 88, 1), pltpu.roll(last, 48, 1)]
                cells = jnp.stack([v.reshape(16, 8, 128) for v in turned], axis=1)
                put(cells.reshape(384, 128), u, [(3, 0)])

    def gather(rows):
        for i in rows:
            row = jnp.clip(first - 2 + i, 0, 63)
            shifts = [shift_ref[j, row] + 12 for j in range(3)]

            def group(x, c, i=i, shifts=shifts):
                out = []
                for b in range(3):
                    x0, x1, x2 = [x_ref[i, lax.rem(3 * x + b + s, 12)] for s in shifts]
                    out.append(jnp.concatenate([jnp.where(left40, x0, x1), x2], axis=1))
                lhs_ref[x, :, 256 * i : 256 * i + 256] = jnp.concatenate(out, axis=0).astype(BF16)
                return c

            lax.fori_loop(0, 4, group, 0)

    turn(lambda u: r_ref[u : u + 16], 2, (0, 1, 2, 3))
    own_w.wait()
    for d in range(1, 8):
        y_copy(d, 8 * own_x + lax.rem(own_y + 8 - d, 8)).wait_recv()
    for d in range(1, 4):
        w_go(x_block(d, own_x))
    gather((2, 3, 4, 5))

    def above(n, start):
        return lax.rem(start + 2 * n, NLAT)

    def below(n, start):
        return lax.rem(start + 2 * NLAT - 2 * n, NLAT)

    def exists(at, part):
        if part == 0:
            return at < NLAT - 1
        return (lax.rem(at, 2) == 0) | (at == 11) | (at == 13)

    started = []

    def go(at, part, make):
        make().start()
        started.append((at, part, make))

    def ring(way, n, part):
        place = ga_ref.at[(below, above)[way](n, lat), part]
        slot = 8 * way + 2 * n + part
        to = {"lat": (up2, down2)[way]}
        return remote(place, place, c_send.at[slot], c_recv.at[slot], to)

    def to_twin(slot, at, part):
        place = ga_ref.at[at, part]
        n = 2 * slot + part
        return remote(place, place, s_send.at[n], s_recv.at[n], {"lat": twin})

    def ring_step(n):
        for way in range(2):
            for part in range(2):
                if n == 4 and part != way:
                    continue
                at = (below, above)[way](n, lat)

                @pl.when(exists(at, part))
                def _():
                    place = ga_ref.at[at, part]
                    slot = 8 * way + 2 * (n - 1) + part
                    remote(
                        place, place, c_send.at[slot], c_recv.at[slot], {"lat": (up2, down2)[way]}
                    ).wait_recv()
                    if n < 3 or (n == 3 and part == way):
                        go(at, part, functools.partial(ring, way, n, part))
                    spot = n if way == 0 or n == 4 else 4 + n
                    go(at, part, functools.partial(to_twin, spot, at, part))

    k_up.wait_recv()
    k_down.wait_recv()

    def halo_rows(k, c):
        for side in range(2):
            for n in range(2):
                at = 256 * (6 * side + n)
                rhs_ref[k, at : at + 192] = jnp.dot(
                    kh_ref[side, k, n], sq_ref[side], preferred_element_type=F32
                ).astype(BF16)
        return c

    lax.fori_loop(0, 5, halo_rows, 0)

    h_up.wait_recv()
    h_down.wait_recv()
    for d in range(1, 4):
        x_block(d, lax.rem(own_x + 4 - d, 4)).wait_recv()
    whole = exists(lat, 1)
    even, odds = g_ref[0].astype(F32), g_ref[1]
    ga_ref[lat, 0] = jnp.where(whole, even, even + odds.astype(F32)).astype(BF16)
    ga_ref[lat, 1] = odds
    for part in range(2):

        @pl.when(exists(lat, part))
        def _():
            for way in range(2):
                go(lat, part, functools.partial(ring, way, 0, part))
            go(lat, part, functools.partial(to_twin, 0, lat, part))


    turn(lambda u: rh_ref[0, u : u + 16], -2, (2, 3))
    turn(lambda u: rh_ref[1, u : u + 16], 6, (0, 1))
    gather((0, 1, 6, 7))
    tail = jnp.zeros((8, 32), F32)
    own_a = pltpu.make_async_copy(a_ref.at[lon], ra_ref.at[lon], own_sem.at[3])
    own_b = pltpu.make_async_copy(b_ref.at[lon], rb_ref.at[lon], own_sem.at[8])
    for step in range(4):
        x = lax.rem(own_x + step, 4)

        def basis(k, c, x=x):
            acc_ref[k] = jnp.dot(lhs_ref[x], rhs_ref[k], preferred_element_type=F32)
            return c

        lax.fori_loop(0, 5, basis, 0)
        for y in range(8):
            groups = [divmod(3 * y + n, 8) for n in range(3)]
            parts = []
            for k in range(5):
                n = 0
                while n < 3:
                    beta, qg = groups[n]
                    m = n
                    while m < 3 and groups[m][0] == beta:
                        m += 1
                    parts.append(
                        acc_ref[k, 40 * beta : 40 * beta + 40, 32 * qg : 32 * (qg + m - n)]
                    )
                    n = m
            value = jnp.concatenate(parts, axis=1)
            a_ref[8 * x + y] = value[:, 0:384].astype(BF16)
            last = value[:, 384:480]
            side = [last[32:40, 32 * n : 32 * n + 32] for n in range(3)]
            side = jnp.concatenate(side + [tail], axis=0)
            b_ref[8 * x + y] = jnp.concatenate([last[0:32], side], axis=1).astype(BF16)

        def start_a(n, c, x=x, step=step):
            to = 8 * x + lax.rem(own_y + n, 8)
            send_a(to, step).start()
            send_b(to, step).start()
            return c

        lax.fori_loop(1 if step == 0 else 0, 8, start_a, 0)
        if step == 0:
            own_a.start()
            own_b.start()
        elif step == 1:
            ring_step(1)
    for n in range(2, 5):
        ring_step(n)

    for slot in range(8):
        at = below(slot, twin) if slot < 5 else above(slot - 4, twin)
        for part in range(2):

            @pl.when(exists(at, part))
            def _():
                to_twin(slot, at, part).wait_recv()

    for k in range(5):

        def order(x, c, k=k):
            def cut(at, part):
                return ga_ref[at, part, pl.ds(4 * x, 4)].astype(F32)

            one, two = FULL[2 * k], FULL[2 * k + 1]
            w = jnp.stack(
                [cut(one, 0), cut(two, 0), cut(2 * k + 1, 0), cut(one, 1), cut(two, 1)], axis=1
            )
            w = jnp.concatenate([w.reshape(160, 640), jnp.zeros((96, 640), F32)], axis=0)
            wv_ref[x, 256 * k : 256 * k + 256] = w.astype(BF16)
            return c

        lax.fori_loop(0, 4, order, 0)

    for step in range(4):
        x = lax.rem(own_x + 4 - step, 4)

        count = pl.ds(0, 7 if step == 0 else 8)
        remote(
            a_ref.at[count], ra_ref.at[count], a_send.at[0], a_recv.at[step], {"lon": peer(1)}
        ).wait_recv()
        remote(
            b_ref.at[count], rb_ref.at[count], a_send.at[1], a_recv.at[4 + step], {"lon": peer(1)}
        ).wait_recv()
        if step == 0:
            own_a.wait()
            own_b.wait()
        for e in range(2):
            parts = []
            for g in range(4):
                last = rb_ref[8 * x + 2 * g + e].astype(F32)
                side = [last[8 * n : 8 * n + 8, 96:128] for n in range(3)]
                both = [last[:, 0:96], jnp.concatenate(side, axis=1)]
                wide = [ra_ref[8 * x + 2 * g + e].astype(F32), jnp.concatenate(both, axis=0)]
                parts.append(jnp.concatenate(wide + [jnp.zeros((40, 32), F32)], axis=1))
            turned = jnp.concatenate(parts + [jnp.zeros((96, 512), F32)], axis=0).T.astype(BF16)
            for k in range(5):
                t_ref[96 * e : 96 * e + 96, 256 * k : 256 * k + 256] = turned[
                    96 * k : 96 * k + 96
                ]
        now = jnp.dot(t_ref[...], wv_ref[x], preferred_element_type=F32)
        if step == 0:
            sum_ref[...] = now
        elif step < 3:
            sum_ref[...] += now
        else:
            v = sum_ref[...] + now
            v = (v * (1.0 + lax.erf(v * 0.7071067811865476)) * 0.5).reshape(2, 3, 4, 8, 640)
            for e in range(2):
                for o in range(4):
                    o_ref[e, o] = v[e, :, o].reshape(24, 640).astype(BF16)

    others = pl.ds(0, NLON - 1)
    to = {"lon": peer(1)}
    remote(m_ref.at[others], r_ref.at[others], m_send.at[0], m_recv.at[0], to).wait_send()
    remote(a_ref.at[others], ra_ref.at[others], a_send.at[0], a_recv.at[0], to).wait_send()
    remote(b_ref.at[others], rb_ref.at[others], a_send.at[1], a_recv.at[4], to).wait_send()
    for copy in w_started + [k_up, k_down, h_up, h_down]:
        copy.wait_send()
    for at, part, make in started:

        @pl.when(exists(at, part))
        def _():
            make().wait_send()


def per_device(fields, kernel, band_low, block_shift, mix_weight):
    whole = pl.BlockSpec(memory_space=pltpu.VMEM)
    anywhere = pl.BlockSpec(memory_space=pl.ANY)
    shape = jax.ShapeDtypeStruct
    dma = pltpu.SemaphoreType.DMA
    vmem = pltpu.VMEM

    return pl.pallas_call(
        layer_kernel,
        out_shape=pltpu.VMEM((2, 4, 24, 640), BF16),
        in_specs=[anywhere] * 5,
        out_specs=whole,
        scratch_shapes=[
            pltpu.SMEM((5, 64), jnp.int32),
            pltpu.SMEM((3, 64), jnp.int32),
            vmem((2, 4, 24, 640), BF16),
            vmem((5, 20, 640), BF16),
            vmem((5, 4, 3, 3, 64, 64), BF16),
            vmem((32, 32, 128), BF16),
            vmem((16, 8, 640), BF16),
            vmem((32, 32, 128), BF16),
            vmem((2, 32, 32, 128), BF16),
            vmem((2, 16, 8, 640), BF16),
            vmem((2, 5, 2, 192, 128), BF16),
            vmem((2, 5, 2, 192, 128), BF16),
            vmem((8, 12, 40, 128), F32),
            vmem((4, 120, 2048), BF16),
            vmem((5, 2048, 256), BF16),
            vmem((5, 120, 256), F32),
            vmem((32, 40, 384), BF16),
            vmem((32, 32, 128), BF16),
            vmem((5, 64, 256), BF16),
            vmem((2, 128, 256), BF16),
            vmem((32, 40, 384), BF16),
            vmem((32, 32, 128), BF16),
            vmem((16, 2, 16, 8, 640), BF16),
            vmem((4, 1280, 640), BF16),
            vmem((192, 1280), BF16),
            vmem((192, 640), F32),
            dma((1,)), dma((32,)), dma((8,)), dma((8,)), dma((4,)), dma((4,)),
            dma((2,)), dma((8,)), dma((2,)), dma((2,)), dma((2,)), dma((2,)),
            dma((16,)), dma((16,)), dma((16,)), dma((16,)), dma((9,)),
        ],
        compiler_params=pltpu.CompilerParams(collective_id=0, has_side_effects=True),
        name="layer",
    )(
        band_low,
        block_shift.T,
        jnp.transpose(fields, (0, 1, 3, 2)),
        mix_weight,
        kernel,
    )

def solution(mesh):
    placed = (
        P(None, "lat", None, "lon"),
        P(None, "lat", None, None, None, None),
        P(),
        P(),
        P(None, "lon", None),
    )
    return jax.shard_map(
        per_device,
        mesh=mesh,
        in_specs=placed,
        out_specs=P(None, "lat", "lon", None),
        check_vma=False,
    )
```
